32 devices in a mesh: region: 1, band: 32 (over z, y, x, core), tile: 1, sub: 1.
Axes of the slice: x: 2, y: 2, z: 4, core: 2. Of those that a mesh axis runs over, the one named last changes fastest.
Arguments:
- scenes: bfloat16 [60, 6, 1024, 128], P(('region', 'tile'), 'sub', 'band'), may hold values from -6 to 6
- clear_bits: int32 [2, 32, 256], P(('region', 'tile'), 'band'), may hold values from 0 to 1073741823
- footprint: int32 [60, 2], P(('region', 'tile')), may hold values from 0 to 31, as said below
- offsets: int32 [60, 2], P(('region', 'tile')), may hold values from 0 to 15
- acq_day: int32 [60], P(('region', 'tile')), may hold values from 0 to 364
Outputs:
- coefficients: float32 [8, 6, 128, 1024], P('region', 'sub', 'band', 'tile')
- monthly: float32 [12, 6, 128, 1024], P(('region', 'tile'), 'sub', 'band')
- annual: float32 [6, 128, 1024], P(('region', 'sub'), 'band', 'tile')
The draws below stay inside these ranges and needn't reach their ends.
Inputs may be any that keep to these rules, and one draw needn't show every extreme that they name: `clear_bits`: bit j (j < 30) of word w at cell (b, a) is 1 when date 30 w + j is clear over columns 4 b to 4 b + 3 and rows 4 a to 4 a + 3. footprint[t, 0] <= footprint[t, 1]; date t's scene covers columns 4 * footprint[t, 0] to 4 * (footprint[t, 1] + 1) - 1. `offsets`: offsets in sixteenths of a pixel, along rows then columns.
All inputs are finite; a program needn't handle non-finite values.
Results may differ from the reference program's by a relative error of at most 0.005.
Values may be sent and summed in bfloat16 or wider, within the bound.
A program may use at most 64 MiB of HBM per device.

```python
import jax
import jax.numpy as jnp
from jax import lax

SPEC = 6
COLS_DEV = 4
DATES = 60
ROWS = 1024
COLS = 128
WORDS = 2


def draw_footprint(key, part):
    strip_count = COLS // COLS_DEV
    first_key, span_key = jax.random.split(jax.random.fold_in(key, 11))
    first_strip = jax.random.randint(first_key, (DATES,), 0, strip_count // 2 + 1)
    span_strip = jax.random.randint(span_key, (DATES,), strip_count // 4, strip_count)
    last_strip = jnp.minimum(first_strip + span_strip, strip_count - 1)
    return jnp.stack([first_strip, last_strip], axis=1).astype(jnp.int32)


def draw_acq_day(key, part):
    return jax.random.randint(jax.random.fold_in(key, 23), (DATES,), 0, 365).astype(jnp.int32)


def set_ends(result, own_key, low, high):
    longest = result.shape.index(max(result.shape))
    spots = []
    for shift in (0, 1):
        where = [jax.random.randint(jax.random.fold_in(own_key, axis), (), 0, length) for axis, length in enumerate(result.shape)]
        where[longest] = (where[longest] + shift) % result.shape[longest]
        spots.append(tuple(where))
    return result.at[spots[0]].set(low).at[spots[1]].set(high)


def levels(key, extent, cuts, least, high):
    loudness, own = 1.0, jax.random.fold_in(key, 6)
    for axis_at, blocks in cuts:
        steps = jnp.exp(jax.random.uniform(jax.random.fold_in(own, axis_at), (blocks,), jnp.float32, least / len(cuts), high / len(cuts)))
        loudness = loudness * jnp.repeat(steps, extent[axis_at] // blocks).reshape([-1 if axis == axis_at else 1 for axis in range(len(extent))])
    return loudness


def bell_draw(stream_key, extent, width, reach, cuts=(), kind=jnp.bfloat16):
    level = levels(stream_key, extent, cuts, -0.22, 0.18) if cuts else 1.0
    values = jax.random.normal(stream_key, extent, jnp.float32) * width * level
    return jnp.minimum(jnp.maximum(values, -reach), reach).astype(kind)


def setup_inputs(seed: int = 0, part: int = 0) -> dict:
    keys = jax.random.split(jax.random.key(seed), 6)
    part_splits = jax.random.split(jax.random.fold_in(keys[5], part), 6)
    return {
        "scenes": bell_draw(part_splits[0], (DATES, SPEC, ROWS, COLS), 1.0, 6.0, ((2, 32),)),
        "clear_bits": set_ends(jax.random.randint(part_splits[1], (WORDS, COLS // 4, ROWS // 4), 0, 1073741824), jax.random.fold_in(part_splits[1], 1), 0, 1073741823).astype(jnp.int32),
        "footprint": draw_footprint(jax.random.fold_in(jax.random.fold_in(keys[5], part), 71), part),
        "offsets": set_ends(jax.random.randint(part_splits[3], (DATES, 2), 0, 16), jax.random.fold_in(part_splits[3], 1), 0, 15).astype(jnp.int32),
        "acq_day": draw_acq_day(jax.random.fold_in(jax.random.fold_in(keys[5], part), 71), part),
    }


RIDGE = 1.0

def design_tables(acq_day):
    day_phase = acq_day.astype(jnp.float32) / 365.0
    columns = [jnp.ones_like(day_phase), 2.0 * day_phase - 1.0]
    for harmonic in (1, 2, 3):
        turn_angle = 2.0 * jnp.pi * harmonic * day_phase
        columns = columns + [jnp.cos(turn_angle), jnp.sin(turn_angle)]
    harmonic_basis = jnp.stack(columns, axis=1)
    month_index = acq_day * 12 // 365
    onehot = (month_index[:, None] == jnp.arange(12, dtype=jnp.int32)[None, :]).astype(jnp.float32)
    products = jnp.stack([harmonic_basis[:, row_term] * harmonic_basis[:, col_term] for row_term in range(8) for col_term in range(row_term + 1)], axis=1)
    return (jnp.concatenate([products, onehot], axis=1), jnp.concatenate([harmonic_basis, onehot], axis=1))

def bilinear(padded, offsets):
    shift_row = (offsets[:, 0].astype(jnp.float32) / 16.0)[:, None, None, None]
    shift_col = (offsets[:, 1].astype(jnp.float32) / 16.0)[:, None, None, None]
    upper_rows = padded[:, :, :-1].astype(jnp.float32)
    lower_rows = padded[:, :, 1:].astype(jnp.float32)

    def across(source):
        right_cell = jnp.concatenate([source[..., 1:], jnp.zeros_like(source[..., :1])], axis=-1)
        return (1.0 - shift_col) * source + shift_col * right_cell
    return ((1.0 - shift_row) * across(upper_rows) + shift_row * across(lower_rows)).astype(jnp.bfloat16)

def clear_weight(cell_words, footprint, col_start, strip_width):
    date_count = footprint.shape[0]
    per_date = jnp.repeat(cell_words, 30, axis=0)
    bit_place = (jnp.arange(date_count, dtype=jnp.int32) % 30)[:, None, None]
    clear_flag = jnp.right_shift(per_date, bit_place) & 1
    pixel_flag = jnp.repeat(jnp.repeat(clear_flag, 4, axis=1), 4, axis=2)
    strip_index = (col_start + jnp.arange(pixel_flag.shape[1], dtype=jnp.int32)) // strip_width
    covered = (strip_index[None, :] >= footprint[:, 0:1]) & (strip_index[None, :] <= footprint[:, 1:2])
    return pixel_flag.astype(jnp.float32) * covered[:, :, None].astype(jnp.float32)

def partial_sums(weight, values, common_table, banded_table):
    common = jnp.einsum('dxy,dk->kxy', weight, common_table, precision=lax.Precision.HIGHEST)
    weighted = values.astype(jnp.float32) * weight[:, None]
    banded = jnp.einsum('dsxy,dk->ksxy', weighted, banded_table, precision=lax.Precision.HIGHEST)
    return (common, banded)

def solve_normal(gram, rhs):
    pair_list = [(row_term, col_term) for row_term in range(8) for col_term in range(row_term + 1)]
    gram_entry = {}
    for position, term_pair in enumerate(pair_list):
        gram_entry[term_pair] = gram[position]
    factor = {}
    for col_term in range(8):
        pivot_value = gram_entry[col_term, col_term] + RIDGE
        for inner_term in range(col_term):
            pivot_value = pivot_value - factor[col_term, inner_term] * factor[col_term, inner_term]
        diag_root = jnp.sqrt(pivot_value)
        factor[col_term, col_term] = diag_root
        for row_term in range(col_term + 1, 8):
            running = gram_entry[row_term, col_term]
            for inner_term in range(col_term):
                running = running - factor[row_term, inner_term] * factor[col_term, inner_term]
            factor[row_term, col_term] = running / diag_root
    forward = []
    for row_term in range(8):
        running = rhs[row_term]
        for inner_term in range(row_term):
            running = running - factor[row_term, inner_term] * forward[inner_term]
        forward.append(running / factor[row_term, row_term])
    backward = [forward[0]] * 8
    for row_term in reversed(range(8)):
        running = forward[row_term]
        for inner_term in range(row_term + 1, 8):
            running = running - factor[inner_term, row_term] * backward[inner_term]
        backward[row_term] = running / factor[row_term, row_term]
    return jnp.stack(backward, axis=0)

def smooth_axis(padded_field, along):
    inner_size = padded_field.shape[along] - 2
    left_part = lax.slice_in_dim(padded_field, 0, inner_size, axis=along)
    centre_part = lax.slice_in_dim(padded_field, 1, inner_size + 1, axis=along)
    right_part = lax.slice_in_dim(padded_field, 2, inner_size + 2, axis=along)
    return 0.25 * left_part + 0.5 * centre_part + 0.25 * right_part

def reference(scenes, clear_bits, footprint, offsets, acq_day):
    padded = jnp.concatenate([scenes, jnp.zeros_like(scenes[:, :, 0:1, :])], axis=2)
    resampled = jnp.swapaxes(bilinear(padded, offsets), 2, 3)
    weight = clear_weight(clear_bits, footprint, 0, COLS_DEV)
    common_table, banded_table = design_tables(acq_day)
    common, banded = partial_sums(weight, resampled, common_table, banded_table)
    gram = common[:36]
    month_count = common[36:]
    rhs = banded[:8]
    month_sum = banded[8:]
    coefficients = solve_normal(gram, rhs)
    composite = month_sum / jnp.maximum(month_count, 1.0)[:, None]
    yearly = lax.optimization_barrier(jnp.sum(month_sum, axis=0)) / jnp.maximum(lax.optimization_barrier(jnp.sum(month_count, axis=0)), 1.0)
    month_pad = jnp.pad(composite, ((0, 0), (0, 0), (1, 1), (1, 1)))
    monthly = smooth_axis(smooth_axis(month_pad, 3), 2)
    year_pad = jnp.pad(yearly, ((0, 0), (1, 1), (1, 1)))
    annual = smooth_axis(smooth_axis(year_pad, 2), 1)
    return (coefficients, monthly, annual)
```

```python
import functools

import jax
import jax.numpy as jnp
from jax import lax
from jax.experimental import pallas as pl
from jax.experimental.pallas import tpu as pltpu
from jax.sharding import PartitionSpec as P

RIDGE = 1.0


def shifted(value, axis, steps):
    count = lax.axis_size(axis)
    first, last = (max(0, -steps), min(count, count - steps))
    return lax.ppermute(value, axis, [(source, source + steps) for source in range(first, last)])


def extended(x, sides, width):
    for axis, dim in sides:
        devices, length = (lax.axis_size(axis), x.shape[dim])
        up = [(i, (i + 1) % devices) for i in range(devices - 1)]
        down = [(j, i) for i, j in up]
        last = lax.slice_in_dim(x, length - width, length, axis=dim)
        first = lax.slice_in_dim(x, 0, width, axis=dim)
        before = lax.ppermute(last, axis, up)
        after = lax.ppermute(first, axis, down)
        x = jnp.concatenate([before, x, after], axis=dim)
    return x


def design_tables(acq_day):
    day_phase = acq_day.astype(jnp.float32) / 365.0
    columns = [jnp.ones_like(day_phase), 2.0 * day_phase - 1.0]
    for harmonic in (1, 2, 3):
        turn_angle = 2.0 * jnp.pi * harmonic * day_phase
        columns = columns + [jnp.cos(turn_angle), jnp.sin(turn_angle)]
    harmonic_basis = jnp.stack(columns, axis=1)
    month_index = acq_day * 12 // 365
    onehot = (month_index[:, None] == jnp.arange(12, dtype=jnp.int32)[None, :]).astype(jnp.float32)
    products = jnp.stack(
        [
            harmonic_basis[:, row_term] * harmonic_basis[:, col_term]
            for row_term in range(8)
            for col_term in range(row_term + 1)
        ],
        axis=1,
    )
    return (
        jnp.concatenate([products, onehot], axis=1),
        jnp.concatenate([harmonic_basis, onehot], axis=1),
    )


def bilinear(padded, offsets):
    shift_row = (offsets[:, 0].astype(jnp.float32) / 16.0)[:, None, None, None]
    shift_col = (offsets[:, 1].astype(jnp.float32) / 16.0)[:, None, None, None]
    upper_rows = padded[:, :, :-1].astype(jnp.float32)
    lower_rows = padded[:, :, 1:].astype(jnp.float32)

    def across(source):
        right_cell = jnp.concatenate([source[..., 1:], jnp.zeros_like(source[..., :1])], axis=-1)
        return (1.0 - shift_col) * source + shift_col * right_cell

    return ((1.0 - shift_row) * across(upper_rows) + shift_row * across(lower_rows)).astype(
        jnp.bfloat16
    )


def clear_weight(cell_words, footprint, strip_width):
    date_count = footprint.shape[0]
    per_date = jnp.repeat(cell_words, 30, axis=0)
    bit_place = (jnp.arange(date_count, dtype=jnp.int32) % 30)[:, None, None]
    clear_flag = jnp.right_shift(per_date, bit_place) & 1
    pixel_flag = jnp.repeat(jnp.repeat(clear_flag, 4, axis=1), 4, axis=2)
    strip_index = jnp.arange(pixel_flag.shape[1], dtype=jnp.int32) // strip_width
    covered = (strip_index[None, :] >= footprint[:, 0:1]) & (
        strip_index[None, :] <= footprint[:, 1:2]
    )
    return pixel_flag.astype(jnp.float32) * covered[:, :, None].astype(jnp.float32)


def partial_sums(weight, values, common_table, banded_table):
    common = jnp.einsum("dxy,dk->kxy", weight, common_table, precision=lax.Precision.HIGHEST)
    weighted = values.astype(jnp.float32) * weight[:, None]
    banded = jnp.einsum("dsxy,dk->ksxy", weighted, banded_table, precision=lax.Precision.HIGHEST)
    return (common, banded)


def solve_normal(gram, rhs):
    pair_list = [(row_term, col_term) for row_term in range(8) for col_term in range(row_term + 1)]
    gram_entry = {}
    for position, term_pair in enumerate(pair_list):
        gram_entry[term_pair] = gram[position]
    factor = {}
    for col_term in range(8):
        pivot_value = gram_entry[col_term, col_term] + RIDGE
        for inner_term in range(col_term):
            pivot_value = pivot_value - factor[col_term, inner_term] * factor[col_term, inner_term]
        diag_root = jnp.sqrt(pivot_value)
        factor[col_term, col_term] = diag_root
        for row_term in range(col_term + 1, 8):
            running = gram_entry[row_term, col_term]
            for inner_term in range(col_term):
                running = running - factor[row_term, inner_term] * factor[col_term, inner_term]
            factor[row_term, col_term] = running / diag_root
    forward = []
    for row_term in range(8):
        running = rhs[row_term]
        for inner_term in range(row_term):
            running = running - factor[row_term, inner_term] * forward[inner_term]
        forward.append(running / factor[row_term, row_term])
    backward = [forward[0]] * 8
    for row_term in reversed(range(8)):
        running = forward[row_term]
        for inner_term in range(row_term + 1, 8):
            running = running - factor[inner_term, row_term] * backward[inner_term]
        backward[row_term] = running / factor[row_term, row_term]
    return jnp.stack(backward, axis=0)


def smooth_axis(padded_field, along):
    inner_size = padded_field.shape[along] - 2
    left_part = lax.slice_in_dim(padded_field, 0, inner_size, axis=along)
    centre_part = lax.slice_in_dim(padded_field, 1, inner_size + 1, axis=along)
    right_part = lax.slice_in_dim(padded_field, 2, inner_size + 2, axis=along)
    return 0.25 * left_part + 0.5 * centre_part + 0.25 * right_part


def shards(scenes, clear_bits, footprint, offsets, acq_day):
    date_count, band_count, row_local, col_count = scenes.shape
    strip_count = lax.axis_size("band")
    tile_count = lax.axis_size("tile")
    strip_width = col_count // strip_count
    row_count = row_local * strip_count
    common_table, banded_table = design_tables(acq_day)
    below = shifted(scenes[:, :, 0:1, :], "band", -1)
    resampled = bilinear(jnp.concatenate([scenes, below], axis=2), offsets)
    flipped = jnp.swapaxes(resampled, 2, 3)
    cell_words = lax.all_to_all(clear_bits, "band", split_axis=2, concat_axis=1, tiled=True)
    weight = clear_weight(cell_words, footprint, strip_width)
    common, banded = partial_sums(weight, flipped, common_table, banded_table)
    common, banded = (
        lax.all_to_all(common, "band", split_axis=1, concat_axis=2, tiled=True),
        lax.all_to_all(
            banded.reshape(-1, col_count, row_local),
            "band",
            split_axis=1,
            concat_axis=2,
            tiled=True,
        ),
    )
    banded = banded.reshape(20, band_count, strip_width, row_count)
    gram = common[:36]
    month_count = common[36:]
    rhs = banded[:8]
    month_sum = banded[8:]
    annual_sum = jnp.sum(month_sum, axis=0)
    annual_count = jnp.sum(month_count, axis=0)
    month_sum, month_count = (
        lax.psum_scatter(month_sum, "tile", scatter_dimension=0, tiled=True),
        lax.psum_scatter(month_count, "tile", scatter_dimension=0, tiled=True),
    )
    composite = month_sum / jnp.maximum(month_count, 1.0)[:, None]
    month_edged = extended(composite, (("band", 2),), 1)
    month_edged = jnp.pad(month_edged, ((0, 0), (0, 0), (0, 0), (1, 1)))
    monthly = smooth_axis(smooth_axis(month_edged, 3), 2)
    share = row_count // tile_count
    gram, rhs, annual_sum, annual_count = lax.psum((gram, rhs, annual_sum, annual_count), "tile")
    start = lax.axis_index("tile") * share
    gram = lax.dynamic_slice_in_dim(gram, start, share, 2)
    rhs = lax.dynamic_slice_in_dim(rhs, start, share, 3)
    annual_sum = lax.dynamic_slice_in_dim(annual_sum, start, share, 2)
    annual_count = lax.dynamic_slice_in_dim(annual_count, start, share, 1)
    coefficients = solve_normal(gram, rhs)
    yearly = annual_sum / jnp.maximum(annual_count, 1.0)
    year_edged = extended(yearly, (("band", 1), ("tile", 2)), 1)
    annual = smooth_axis(smooth_axis(year_edged, 2), 1)
    return (coefficients, monthly, annual)


def fit_kernel(dates, bands, off, bas, scenes_ref, w8_ref, hu_ref, tab_ref, out_ref, mix, mix_last, wide, fac, stack, planes):
    f32, bf16 = jnp.float32, jnp.bfloat16
    step = pl.program_id(0)
    sub8 = lax.broadcasted_iota(jnp.int32, (8, 128), 0)
    upper = sub8 < 4
    depth = dates * 8

    def spread(cell, rb):
        return jnp.where(upper, cell[2 * rb : 2 * rb + 1, :], cell[2 * rb + 1 : 2 * rb + 2, :])

    @pl.when(step == 0)
    def _():
        pick = (lax.broadcasted_iota(jnp.int32, (224, 32), 0) // 8 == lax.broadcasted_iota(jnp.int32, (224, 32), 1)).astype(f32).astype(bf16)
        tab = jnp.dot(pick, tab_ref[...], preferred_element_type=f32)
        last = lax.broadcasted_iota(jnp.int32, (224, 64), 0) % 8 == 7
        mix_last[...] = jnp.where(last, tab, 0.0).astype(bf16)
        place = (lax.broadcasted_iota(jnp.int32, (64, depth), 1) // 8 == lax.broadcasted_iota(jnp.int32, (64, depth), 0)).astype(f32).astype(bf16)
        full = jnp.dot(tab.astype(bf16), place, preferred_element_type=f32)
        same = lax.broadcasted_iota(jnp.int32, (224, depth), 0) % 8 == lax.broadcasted_iota(jnp.int32, (224, depth), 1) % 8
        mix[...] = jnp.where(same, full, 0.0).astype(bf16)
        planes[pl.ds(bands * 21 * 32, 64), :] = jnp.zeros((64, 128), f32)

        def date(t, acc):
            w = w8_ref[t]
            for rb in range(4):
                wide[t, pl.ds(8 * rb, 8), :] = spread(w, rb)
            b = [bas[t * 20 + i] for i in range(20)]
            out = []
            for i in range(8):
                wb = w * b[i]
                for j in range(i + 1):
                    out.append(acc[len(out)] + wb * b[j])
            for m in range(12):
                out.append(acc[len(out)] + w * b[8 + m])
            return tuple(out)

        acc = lax.fori_loop(0, dates, date, tuple(jnp.zeros((8, 128), f32) for _ in range(48)))
        gram = {}
        for i in range(8):
            for j in range(i + 1):
                gram[i, j] = acc[i * (i + 1) // 2 + j]
        low, inv = {}, {}
        for j in range(8):
            pivot = gram[j, j] + RIDGE
            for k in range(j):
                pivot = pivot - low[j, k] * low[j, k]
            inv[j] = 1.0 / jnp.sqrt(pivot)
            for i in range(j + 1, 8):
                run = gram[i, j]
                for k in range(j):
                    run = run - low[i, k] * low[j, k]
                low[i, j] = run * inv[j]
        items = [inv[i] for i in range(8)]
        items += [low[i, j] for i in range(8) for j in range(i)]
        items += [1.0 / jnp.maximum(acc[36 + m], 1.0) for m in range(12)]
        total = acc[36]
        for m in range(1, 12):
            total = total + acc[36 + m]
        items.append(1.0 / jnp.maximum(total, 1.0))
        for n, item in enumerate(items):
            for rb in range(4):
                fac[n, pl.ds(8 * rb, 8), :] = spread(item, rb)

    lane = lax.broadcasted_iota(jnp.int32, (32, 128), 1)
    row = lax.broadcasted_iota(jnp.int32, (32, 128), 0)

    def pair(p, carry):
        u = []
        for t2 in range(2):
            t = 2 * p + t2
            fy = off[2 * t].astype(f32) * 0.0625
            fx = off[2 * t + 1].astype(f32) * 0.0625
            x = scenes_ref[t, 0].astype(f32)
            xb = (1.0 - fx) * x + jnp.where(lane < 127, fx, 0.0) * pltpu.roll(x, 127, 1)
            v = (1.0 - fy) * xb + jnp.where(row < 31, fy, 0.0) * pltpu.roll(xb, 31, 0)
            u.append(v * wide[t])
        for rb in range(4):
            both = jnp.concatenate([u[0][8 * rb : 8 * rb + 8], u[1][8 * rb : 8 * rb + 8]], axis=0)
            stack[rb // 2, pl.ds(pl.multiple_of(16 * p, 16), 16), pl.ds(128 * (rb % 2), 128)] = both.astype(bf16)
        return carry

    lax.fori_loop(0, dates // 2, pair, 0, unroll=2)
    sums = [jnp.dot(mix[...], stack[h], preferred_element_type=f32) for h in range(2)]
    extra = jnp.dot(mix_last[...], hu_ref[0], preferred_element_type=f32)
    lane8 = lax.broadcasted_iota(jnp.int32, (8, 128), 1)
    ends = jnp.where(lane8 > 0, 0.25, 0.0), jnp.where(lane8 < 127, 0.25, 0.0)

    def smooth(x):
        return 0.5 * x + ends[0] * pltpu.roll(x, 1, 1) + ends[1] * pltpu.roll(x, 127, 1)

    for rb in range(4):
        rows = pl.ds(8 * rb, 8)

        def term(n):
            part = sums[rb // 2][8 * n : 8 * n + 8, 128 * (rb % 2) : 128 * (rb % 2) + 128]
            return part + extra[8 * n : 8 * n + 8] if rb == 3 else part

        def low(i, j):
            return fac[8 + i * (i - 1) // 2 + j, rows, :]

        def put(n, value):
            at = pl.multiple_of((step * 21 + n) * 32 + 8 * rb, 8)
            planes[pl.ds(at, 8), :] = value

        fwd = []
        for i in range(8):
            run = term(i) + term(8 + i)
            for k in range(i):
                run = run - low(i, k) * fwd[k]
            fwd.append(run * fac[i, rows, :])
        back = [None] * 8
        for i in reversed(range(8)):
            run = fwd[i]
            for k in range(i + 1, 8):
                run = run - low(k, i) * back[k]
            back[i] = run * fac[i, rows, :]
            put(i, back[i])
        total = None
        for m in range(12):
            month = term(16 + m)
            total = month if total is None else total + month
            put(8 + m, smooth(month * fac[36 + m, rows, :]))
        put(20, smooth(total * fac[48, rows, :]))

    @pl.when(step == bands - 1)
    def _():
        first = lax.broadcasted_iota(jnp.int32, (16, 8, 128), 1) < 4

        def group(gg, carry):
            halves = []
            for h in range(2):
                a, b = [
                    planes[pl.ds(pl.multiple_of((4 * gg + 2 * h + k) * 128, 128), 128), :].T.reshape(16, 8, 128)
                    for k in range(2)
                ]
                halves.append((jnp.where(first, a, pltpu.roll(b, 4, 1)), jnp.where(first, pltpu.roll(a, 4, 1), b)))
            for which in range(2):
                out_ref[:, which, pl.ds(pl.multiple_of(16 * gg, 16), 16), :] = jnp.concatenate(
                    [halves[0][which], halves[1][which]], axis=1
                ).astype(bf16)
            return carry

        lax.fori_loop(0, out_ref.shape[2] // 16, group, 0)


def lay_kernel(bands, recv, coef, monthly, annual):
    f32 = jnp.float32
    strips = recv.shape[0]
    quads = strips // 4
    width = strips * 32
    lane = lax.broadcasted_iota(jnp.int32, (8, 128), 1)
    even = (lane // 32) % 2 == 0
    front = lane < 64
    wide = lax.broadcasted_iota(jnp.int32, (8, width), 1)

    def swap(a, b, mask, shift):
        return jnp.where(mask, a, pltpu.roll(b, shift, 1)), jnp.where(mask, pltpu.roll(a, 128 - shift, 1), b)

    for gg in range(recv.shape[1] // 8):
        rows = [[], [], [], []]
        for q in range(quads):
            v = [recv[4 * q + j, pl.ds(8 * gg, 8), :].astype(f32) for j in range(4)]
            a0, a1 = swap(v[0], v[1], even, 32)
            a2, a3 = swap(v[2], v[3], even, 32)
            o0, o2 = swap(a0, a2, front, 64)
            o1, o3 = swap(a1, a3, front, 64)
            for p, o in enumerate((o0, o1, o2, o3)):
                rows[p].append(o)
        for p in range(4):
            full = jnp.concatenate(rows[p], axis=1)
            where_to = [divmod(4 * (2 * gg + half) + p, 21) for half in range(2)]
            if any(s < bands and j >= 8 for s, j in where_to):
                before = jnp.where(wide > 0, pltpu.roll(full, 1, 1), 0.0)
                after = jnp.where(wide < width - 1, pltpu.roll(full, width - 1, 1), 0.0)
                soft = 0.25 * before + 0.5 * full + 0.25 * after
            for half, (s, j) in enumerate(where_to):
                if s >= bands:
                    continue
                part = slice(4 * half, 4 * half + 4)
                if j < 8:
                    coef[j, s] = full[part]
                elif j < 20:
                    monthly[j - 8, s] = soft[part]
                else:
                    annual[s] = soft[part]


def fast(scenes, clear_bits, footprint, offsets, acq_day):
    f32, bf16 = jnp.float32, jnp.bfloat16
    dates, bands, rows, cols = scenes.shape
    strips = lax.axis_size("band")
    strip_width = cols // strips
    halo = shifted(scenes[:, :, 0, :], "band", -1)
    words = lax.all_to_all(clear_bits, "band", split_axis=2, concat_axis=1, tiled=True)
    _, table = design_tables(acq_day)
    high = table.astype(bf16)
    low = (table[:, :8] - high[:, :8].astype(f32)).astype(bf16)
    tab = jnp.concatenate([high[:, :8], low, high[:, 8:]], axis=1).T
    tab = jnp.pad(tab, ((0, 4), (0, 64 - dates)))
    cells = jnp.swapaxes(words, 1, 2)
    flags = (jnp.repeat(cells, 30, axis=0)[:dates] >> (jnp.arange(dates, dtype=jnp.int32) % 30)[:, None, None]) & 1
    strip = jnp.arange(strips, dtype=jnp.int32)
    seen = (strip[None] >= footprint[:, 0:1]) & (strip[None] <= footprint[:, 1:2])
    w8 = jnp.repeat(jnp.where(seen[:, None, :], flags, 0).astype(f32), strip_width, axis=2)
    fy = (offsets[:, 0].astype(f32) / 16.0)[:, None]
    fx = (offsets[:, 1].astype(f32) / 16.0)[:, None, None]
    edge = halo.astype(f32)
    edge = (1.0 - fx) * edge + fx * jnp.pad(edge[..., 1:], ((0, 0), (0, 0), (0, 1)))
    hu = (edge * (fy * w8[:, -1])[:, None, :]).astype(bf16)
    hu = jnp.pad(jnp.swapaxes(hu, 0, 1), ((0, 0), (0, 64 - dates), (0, 0)))
    slots = -(-bands * 21 // 16) * 16
    smem = pl.BlockSpec(memory_space=pltpu.SMEM)
    send = pl.pallas_call(
        functools.partial(fit_kernel, dates, bands),
        grid=(bands,),
        out_shape=jax.ShapeDtypeStruct((strips // 2, 2, slots, cols), bf16),
        in_specs=[
            smem,
            smem,
            pl.BlockSpec((dates, 1, rows, cols), lambda s: (0, s, 0, 0)),
            pl.BlockSpec((dates, 8, cols), lambda s: (0, 0, 0)),
            pl.BlockSpec((1, 64, cols), lambda s: (s, 0, 0)),
            pl.BlockSpec((32, 64), lambda s: (0, 0)),
        ],
        out_specs=pl.BlockSpec((strips // 2, 2, slots, cols), lambda s: (0, 0, 0, 0)),
        scratch_shapes=[
            pltpu.VMEM((224, dates * 8), bf16),
            pltpu.VMEM((224, 64), bf16),
            pltpu.VMEM((dates, rows, cols), f32),
            pltpu.VMEM((49, rows, cols), f32),
            pltpu.VMEM((2, dates * 8, 2 * cols), bf16),
            pltpu.VMEM((slots * rows, cols), f32),
        ],
        compiler_params=pltpu.CompilerParams(dimension_semantics=("arbitrary",), vmem_limit_bytes=48 * 1024 * 1024),
    )(offsets.reshape(-1), table.reshape(-1), scenes, w8, hu, tab)
    recv = exchange(send.reshape(strips, slots, cols))
    vmem = pl.BlockSpec(memory_space=pltpu.VMEM)
    return pl.pallas_call(
        functools.partial(lay_kernel, bands),
        out_shape=(
            jax.ShapeDtypeStruct((8, bands, strip_width, rows * strips), f32),
            jax.ShapeDtypeStruct((12, bands, strip_width, rows * strips), f32),
            jax.ShapeDtypeStruct((bands, strip_width, rows * strips), f32),
        ),
        in_specs=[vmem],
        out_specs=(vmem, vmem, vmem),
        compiler_params=pltpu.CompilerParams(vmem_limit_bytes=32 * 1024 * 1024),
    )(recv)


def exchange(send):
    return lax.all_to_all(send, "band", split_axis=0, concat_axis=0, tiled=True)


def pick(scenes, clear_bits, footprint, offsets, acq_day):
    dates, bands, rows, cols = scenes.shape
    strips = lax.axis_size("band")
    fits = lax.axis_size("tile") == 1 and lax.axis_size("sub") == 1 and strips % 4 == 0
    fits = fits and cols == 128 and rows == 32 and cols == 4 * strips and dates % 2 == 0 and dates <= 64
    return (fast if fits else shards)(scenes, clear_bits, footprint, offsets, acq_day)


def solution(mesh):
    placed = (
        P(("region", "tile"), "sub", "band", None),
        P(("region", "tile"), "band", None),
        P(("region", "tile"), None),
        P(("region", "tile"), None),
        P(("region", "tile")),
    )
    return jax.shard_map(
        pick,
        mesh=mesh,
        in_specs=placed,
        out_specs=(
            P("region", "sub", "band", "tile"),
            P(("region", "tile"), "sub", "band", None),
            P(("region", "sub"), "band", "tile"),
        ),
        check_vma=False,
    )
```

```python
import functools

import jax
import jax.numpy as jnp
from jax import lax
from jax.experimental import pallas as pl
from jax.experimental.pallas import tpu as pltpu
from jax.sharding import PartitionSpec as P

RIDGE = 1.0


def shifted(value, axis, steps):
    count = lax.axis_size(axis)
    first, last = (max(0, -steps), min(count, count - steps))
    return lax.ppermute(value, axis, [(source, source + steps) for source in range(first, last)])


def extended(x, sides, width):
    for axis, dim in sides:
        devices, length = (lax.axis_size(axis), x.shape[dim])
        up = [(i, (i + 1) % devices) for i in range(devices - 1)]
        down = [(j, i) for i, j in up]
        last = lax.slice_in_dim(x, length - width, length, axis=dim)
        first = lax.slice_in_dim(x, 0, width, axis=dim)
        before = lax.ppermute(last, axis, up)
        after = lax.ppermute(first, axis, down)
        x = jnp.concatenate([before, x, after], axis=dim)
    return x


def design_tables(acq_day):
    day_phase = acq_day.astype(jnp.float32) / 365.0
    columns = [jnp.ones_like(day_phase), 2.0 * day_phase - 1.0]
    for harmonic in (1, 2, 3):
        turn_angle = 2.0 * jnp.pi * harmonic * day_phase
        columns = columns + [jnp.cos(turn_angle), jnp.sin(turn_angle)]
    harmonic_basis = jnp.stack(columns, axis=1)
    month_index = acq_day * 12 // 365
    onehot = (month_index[:, None] == jnp.arange(12, dtype=jnp.int32)[None, :]).astype(jnp.float32)
    products = jnp.stack(
        [
            harmonic_basis[:, row_term] * harmonic_basis[:, col_term]
            for row_term in range(8)
            for col_term in range(row_term + 1)
        ],
        axis=1,
    )
    return (
        jnp.concatenate([products, onehot], axis=1),
        jnp.concatenate([harmonic_basis, onehot], axis=1),
    )


def bilinear(padded, offsets):
    shift_row = (offsets[:, 0].astype(jnp.float32) / 16.0)[:, None, None, None]
    shift_col = (offsets[:, 1].astype(jnp.float32) / 16.0)[:, None, None, None]
    upper_rows = padded[:, :, :-1].astype(jnp.float32)
    lower_rows = padded[:, :, 1:].astype(jnp.float32)

    def across(source):
        right_cell = jnp.concatenate([source[..., 1:], jnp.zeros_like(source[..., :1])], axis=-1)
        return (1.0 - shift_col) * source + shift_col * right_cell

    return ((1.0 - shift_row) * across(upper_rows) + shift_row * across(lower_rows)).astype(
        jnp.bfloat16
    )


def clear_weight(cell_words, footprint, strip_width):
    date_count = footprint.shape[0]
    per_date = jnp.repeat(cell_words, 30, axis=0)
    bit_place = (jnp.arange(date_count, dtype=jnp.int32) % 30)[:, None, None]
    clear_flag = jnp.right_shift(per_date, bit_place) & 1
    pixel_flag = jnp.repeat(jnp.repeat(clear_flag, 4, axis=1), 4, axis=2)
    strip_index = jnp.arange(pixel_flag.shape[1], dtype=jnp.int32) // strip_width
    covered = (strip_index[None, :] >= footprint[:, 0:1]) & (
        strip_index[None, :] <= footprint[:, 1:2]
    )
    return pixel_flag.astype(jnp.float32) * covered[:, :, None].astype(jnp.float32)


def partial_sums(weight, values, common_table, banded_table):
    common = jnp.einsum("dxy,dk->kxy", weight, common_table, precision=lax.Precision.HIGHEST)
    weighted = values.astype(jnp.float32) * weight[:, None]
    banded = jnp.einsum("dsxy,dk->ksxy", weighted, banded_table, precision=lax.Precision.HIGHEST)
    return (common, banded)


def solve_normal(gram, rhs):
    pair_list = [(row_term, col_term) for row_term in range(8) for col_term in range(row_term + 1)]
    gram_entry = {}
    for position, term_pair in enumerate(pair_list):
        gram_entry[term_pair] = gram[position]
    factor = {}
    for col_term in range(8):
        pivot_value = gram_entry[col_term, col_term] + RIDGE
        for inner_term in range(col_term):
            pivot_value = pivot_value - factor[col_term, inner_term] * factor[col_term, inner_term]
        diag_root = jnp.sqrt(pivot_value)
        factor[col_term, col_term] = diag_root
        for row_term in range(col_term + 1, 8):
            running = gram_entry[row_term, col_term]
            for inner_term in range(col_term):
                running = running - factor[row_term, inner_term] * factor[col_term, inner_term]
            factor[row_term, col_term] = running / diag_root
    forward = []
    for row_term in range(8):
        running = rhs[row_term]
        for inner_term in range(row_term):
            running = running - factor[row_term, inner_term] * forward[inner_term]
        forward.append(running / factor[row_term, row_term])
    backward = [forward[0]] * 8
    for row_term in reversed(range(8)):
        running = forward[row_term]
        for inner_term in range(row_term + 1, 8):
            running = running - factor[inner_term, row_term] * backward[inner_term]
        backward[row_term] = running / factor[row_term, row_term]
    return jnp.stack(backward, axis=0)


def smooth_axis(padded_field, along):
    inner_size = padded_field.shape[along] - 2
    left_part = lax.slice_in_dim(padded_field, 0, inner_size, axis=along)
    centre_part = lax.slice_in_dim(padded_field, 1, inner_size + 1, axis=along)
    right_part = lax.slice_in_dim(padded_field, 2, inner_size + 2, axis=along)
    return 0.25 * left_part + 0.5 * centre_part + 0.25 * right_part


def shards(scenes, clear_bits, footprint, offsets, acq_day):
    date_count, band_count, row_local, col_count = scenes.shape
    strip_count = lax.axis_size("band")
    tile_count = lax.axis_size("tile")
    strip_width = col_count // strip_count
    row_count = row_local * strip_count
    common_table, banded_table = design_tables(acq_day)
    below = shifted(scenes[:, :, 0:1, :], "band", -1)
    resampled = bilinear(jnp.concatenate([scenes, below], axis=2), offsets)
    flipped = jnp.swapaxes(resampled, 2, 3)
    cell_words = lax.all_to_all(clear_bits, "band", split_axis=2, concat_axis=1, tiled=True)
    weight = clear_weight(cell_words, footprint, strip_width)
    common, banded = partial_sums(weight, flipped, common_table, banded_table)
    common, banded = (
        lax.all_to_all(common, "band", split_axis=1, concat_axis=2, tiled=True),
        lax.all_to_all(
            banded.reshape(-1, col_count, row_local),
            "band",
            split_axis=1,
            concat_axis=2,
            tiled=True,
        ),
    )
    banded = banded.reshape(20, band_count, strip_width, row_count)
    gram = common[:36]
    month_count = common[36:]
    rhs = banded[:8]
    month_sum = banded[8:]
    annual_sum = jnp.sum(month_sum, axis=0)
    annual_count = jnp.sum(month_count, axis=0)
    month_sum, month_count = (
        lax.psum_scatter(month_sum, "tile", scatter_dimension=0, tiled=True),
        lax.psum_scatter(month_count, "tile", scatter_dimension=0, tiled=True),
    )
    composite = month_sum / jnp.maximum(month_count, 1.0)[:, None]
    month_edged = extended(composite, (("band", 2),), 1)
    month_edged = jnp.pad(month_edged, ((0, 0), (0, 0), (0, 0), (1, 1)))
    monthly = smooth_axis(smooth_axis(month_edged, 3), 2)
    share = row_count // tile_count
    gram, rhs, annual_sum, annual_count = lax.psum((gram, rhs, annual_sum, annual_count), "tile")
    start = lax.axis_index("tile") * share
    gram = lax.dynamic_slice_in_dim(gram, start, share, 2)
    rhs = lax.dynamic_slice_in_dim(rhs, start, share, 3)
    annual_sum = lax.dynamic_slice_in_dim(annual_sum, start, share, 2)
    annual_count = lax.dynamic_slice_in_dim(annual_count, start, share, 1)
    coefficients = solve_normal(gram, rhs)
    yearly = annual_sum / jnp.maximum(annual_count, 1.0)
    year_edged = extended(yearly, (("band", 1), ("tile", 2)), 1)
    annual = smooth_axis(smooth_axis(year_edged, 2), 1)
    return (coefficients, monthly, annual)


def fit_kernel(dates, bands, strips, off, foot, day_s, day_v, words, scenes, out,
               scn, hsf, hs, hr, bits, mix, mix_last, wide, w8, tables, edge_x, edge_w, fac, stack, planes, send,
               scene_sem, bit_send, bit_recv, halo_sem, blk_send, blk_recv, own_sem):
    f32, bf16, i32 = jnp.float32, jnp.bfloat16, jnp.int32
    me = lax.axis_index("band")
    sub8 = lax.broadcasted_iota(i32, (8, 128), 0)
    lane8 = lax.broadcasted_iota(i32, (8, 128), 1)
    upper = sub8 < 4
    depth = dates * 8
    load = pltpu.make_async_copy(scenes, scn, scene_sem)
    load.start()

    def at(k):
        return lax.rem(me + k, strips)

    barrier = pltpu.get_barrier_semaphore()

    def greet(k, c):
        pl.semaphore_signal(barrier, inc=1, device_id={"band": at(k)}, device_id_type=pl.DeviceIdType.MESH)
        return c

    lax.fori_loop(1, strips, greet, 0)
    pl.semaphore_wait(barrier, strips - 1)

    def bit_copy(k):
        return pltpu.make_async_remote_copy(
            src_ref=words, dst_ref=bits.at[me], send_sem=bit_send.at[at(k)], recv_sem=bit_recv.at[me],
            device_id={"band": at(k)}, device_id_type=pl.DeviceIdType.MESH)

    def send_bits(k, c):
        bit_copy(k).start()
        return c

    lax.fori_loop(1, strips, send_bits, 0)
    own_bits = pltpu.make_async_copy(words, bits.at[me], own_sem.at[0])
    own_bits.start()

    def basis(day, shape, which):
        u = day.astype(f32) / 365.0
        h = (which // 2).astype(f32)
        wave = jnp.cos((2.0 * jnp.pi) * h * u - jnp.where(which % 2 == 1, 0.5 * jnp.pi, 0.0))
        return jnp.where(which == 0, 1.0, jnp.where(which == 1, 2.0 * u - 1.0, wave))

    d8 = jnp.broadcast_to(day_v[...], (8, 64))
    which8 = lax.broadcasted_iota(i32, (8, 64), 0)
    real = lax.broadcasted_iota(i32, (8, 64), 1) < dates
    b8 = jnp.where(real, basis(d8, (8, 64), which8), 0.0)
    high = b8.astype(bf16).astype(f32)
    d16 = jnp.broadcast_to(day_v[...], (16, 64)) * 12
    m16 = lax.broadcasted_iota(i32, (16, 64), 0)
    ok16 = (lax.broadcasted_iota(i32, (16, 64), 1) < dates) & (m16 < 12)
    hot = jnp.where(ok16 & (d16 >= 365 * m16) & (d16 < 365 * m16 + 365), 1.0, 0.0)
    tab_in = jnp.concatenate([high, b8 - high, hot], axis=0).astype(bf16)
    choose = (lax.broadcasted_iota(i32, (224, 32), 0) // 8 == lax.broadcasted_iota(i32, (224, 32), 1)).astype(f32).astype(bf16)
    tab = jnp.dot(choose, tab_in, preferred_element_type=f32)
    last = lax.broadcasted_iota(i32, (224, 64), 0) % 8 == 7
    mix_last[...] = jnp.where(last, tab, 0.0).astype(bf16)
    place = (lax.broadcasted_iota(i32, (64, depth), 1) // 8 == lax.broadcasted_iota(i32, (64, depth), 0)).astype(f32).astype(bf16)
    full = jnp.dot(tab.astype(bf16), place, preferred_element_type=f32)
    same = lax.broadcasted_iota(i32, (224, depth), 0) % 8 == lax.broadcasted_iota(i32, (224, depth), 1) % 8
    mix[...] = jnp.where(same, full, 0.0).astype(bf16)
    planes[pl.ds(bands * 21 * 32, 64), :] = jnp.zeros((64, 128), f32)
    edge_x[...] = jnp.zeros((64, 128), f32)
    edge_w[...] = jnp.zeros((64, 128), f32)
    hsf[...] = jnp.zeros((bands, 64, 128), f32)

    load.wait()

    def first_rows(t, c):
        for s in range(bands):
            hsf[s, pl.ds(t, 1), :] = scn[t, s, 0:1, :].astype(f32)
        return c

    lax.fori_loop(0, dates, first_rows, 0, unroll=2)
    hs[...] = hsf[...].astype(bf16)
    halo = pltpu.make_async_remote_copy(
        src_ref=hs, dst_ref=hr, send_sem=halo_sem.at[0], recv_sem=halo_sem.at[1],
        device_id={"band": lax.rem(me + strips - 1, strips)}, device_id_type=pl.DeviceIdType.MESH)
    halo.start()

    def take_bits(k, c):
        pltpu.make_async_remote_copy(
            src_ref=words, dst_ref=bits.at[at(k)], send_sem=bit_send.at[at(k)], recv_sem=bit_recv.at[at(k)],
            device_id={"band": at(k)}, device_id_type=pl.DeviceIdType.MESH).wait()
        return c

    lax.fori_loop(1, strips, take_bits, 0)
    own_bits.wait()

    repeat = (lax.broadcasted_iota(i32, (128, strips), 0) // 4 == lax.broadcasted_iota(i32, (128, strips), 1)).astype(f32)
    cells = []
    for w in range(words.shape[0]):
        mine = pltpu.roll(bits[:, w, :], lax.rem(8 * (strips - me), 8 * strips), 1)[:, :128]
        parts = []
        for half in (mine & 32767, mine >> 15):
            spreadc = jnp.dot(repeat, half.astype(f32), precision=lax.Precision.HIGHEST, preferred_element_type=f32)
            parts.append(spreadc.T[0:8].astype(i32))
        cells.append(parts[0] + parts[1] * 32768)

    def spread(cell, rb):
        return jnp.where(upper, cell[2 * rb : 2 * rb + 1, :], cell[2 * rb + 1 : 2 * rb + 2, :])

    acc = tuple(jnp.zeros((8, 128), f32) for _ in range(48))
    for w in range(words.shape[0]):

        def date(j, acc):
            t = 30 * w + j
            seen = (lane8 >= 4 * foot[2 * t]) & (lane8 < 4 * foot[2 * t + 1] + 4)
            wt = jnp.where(seen, (cells[w] >> j) & 1, 0).astype(f32)
            fy = off[2 * t].astype(f32) * 0.0625
            fx = off[2 * t + 1].astype(f32) * 0.0625
            edge_x[pl.ds(t, 1), :] = jnp.full((1, 128), fx)
            edge_w[pl.ds(t, 1), :] = wt[7:8, :] * fy
            for rb in range(4):
                wide[t, pl.ds(8 * rb, 8), :] = spread(wt, rb)
            day = jnp.full((8, 128), day_s[t], i32)
            tables[0] = basis(day, (8, 128), sub8)
            b = [jnp.broadcast_to(tables[0, i : i + 1, :], (8, 128)) for i in range(8)]
            res = []
            for i in range(8):
                wb = wt * b[i]
                for k in range(i + 1):
                    res.append(acc[len(res)] + wb * b[k])
            d12 = day * 12
            for m in range(12):
                res.append(acc[len(res)] + jnp.where((d12 >= 365 * m) & (d12 < 365 * m + 365), wt, 0.0))
            return tuple(res)

        acc = lax.fori_loop(0, min(30, dates - 30 * w), date, acc)
    gram = {}
    for i in range(8):
        for j in range(i + 1):
            gram[i, j] = acc[i * (i + 1) // 2 + j]
    low, inv = {}, {}
    for j in range(8):
        pivot = gram[j, j] + RIDGE
        for k in range(j):
            pivot = pivot - low[j, k] * low[j, k]
        inv[j] = 1.0 / jnp.sqrt(pivot)
        for i in range(j + 1, 8):
            run = gram[i, j]
            for k in range(j):
                run = run - low[i, k] * low[j, k]
            low[i, j] = run * inv[j]
    items = [inv[i] for i in range(8)]
    items += [low[i, j] for i in range(8) for j in range(i)]
    items += [1.0 / jnp.maximum(acc[36 + m], 1.0) for m in range(12)]
    total = acc[36]
    for m in range(1, 12):
        total = total + acc[36 + m]
    items.append(1.0 / jnp.maximum(total, 1.0))
    for n, item in enumerate(items):
        for rb in range(4):
            fac[n, pl.ds(8 * rb, 8), :] = spread(item, rb)

    halo.wait()

    @pl.when(me == strips - 1)
    def _():
        hr[...] = jnp.zeros((bands, 64, 128), bf16)

    lane = lax.broadcasted_iota(i32, (32, 128), 1)
    row = lax.broadcasted_iota(i32, (32, 128), 0)
    lane64 = lax.broadcasted_iota(i32, (64, 128), 1)
    ends = jnp.where(lane8 > 0, 0.25, 0.0), jnp.where(lane8 < 127, 0.25, 0.0)
    first = lax.broadcasted_iota(i32, (16, 8, 128), 1) < 4
    groups = send.shape[2] // 16

    def smooth(x):
        return 0.5 * x + ends[0] * pltpu.roll(x, 1, 1) + ends[1] * pltpu.roll(x, 127, 1)

    def band(s, carry):
        def pair(p, c):
            u = []
            for t2 in range(2):
                t = 2 * p + t2
                fy = off[2 * t].astype(f32) * 0.0625
                fx = off[2 * t + 1].astype(f32) * 0.0625
                x = scn[t, s].astype(f32)
                xb = (1.0 - fx) * x + jnp.where(lane < 127, fx, 0.0) * pltpu.roll(x, 127, 1)
                v = (1.0 - fy) * xb + jnp.where(row < 31, fy, 0.0) * pltpu.roll(xb, 31, 0)
                u.append(v * wide[t])
            for rb in range(4):
                both = jnp.concatenate([u[0][8 * rb : 8 * rb + 8], u[1][8 * rb : 8 * rb + 8]], axis=0)
                stack[rb // 2, pl.ds(pl.multiple_of(16 * p, 16), 16), pl.ds(128 * (rb % 2), 128)] = both.astype(bf16)
            return c

        lax.fori_loop(0, dates // 2, pair, 0, unroll=2)
        e = hr[s].astype(f32)
        fx = edge_x[...]
        hu = ((1.0 - fx) * e + jnp.where(lane64 < 127, fx, 0.0) * pltpu.roll(e, 127, 1)) * edge_w[...]
        sums = [jnp.dot(mix[...], stack[h], preferred_element_type=f32) for h in range(2)]
        extra = jnp.dot(mix_last[...], hu.astype(bf16), preferred_element_type=f32)
        for rb in range(4):
            rows = pl.ds(8 * rb, 8)

            def term(n):
                part = sums[rb // 2][8 * n : 8 * n + 8, 128 * (rb % 2) : 128 * (rb % 2) + 128]
                return part + extra[8 * n : 8 * n + 8] if rb == 3 else part

            def fl(i, j):
                return fac[8 + i * (i - 1) // 2 + j, rows, :]

            def put(n, value):
                start = pl.multiple_of((s * 21 + n) * 32 + 8 * rb, 8)
                planes[pl.ds(start, 8), :] = value

            fwd = []
            for i in range(8):
                run = term(i) + term(8 + i)
                for k in range(i):
                    run = run - fl(i, k) * fwd[k]
                fwd.append(run * fac[i, rows, :])
            back = [None] * 8
            for i in reversed(range(8)):
                run = fwd[i]
                for k in range(i + 1, 8):
                    run = run - fl(k, i) * back[k]
                back[i] = run * fac[i, rows, :]
                put(i, back[i])
            whole = None
            for m in range(12):
                month = term(16 + m)
                whole = month if whole is None else whole + month
                put(8 + m, smooth(month * fac[36 + m, rows, :]))
            put(20, smooth(whole * fac[48, rows, :]))

        def group(gg, c):
            at16 = pl.ds(pl.multiple_of(16 * gg, 16), 16)
            halves = []
            for h in range(2):
                a, b = [
                    planes[pl.ds(pl.multiple_of((4 * gg + 2 * h + k) * 128, 128), 128), :].T.reshape(16, 8, 128)
                    for k in range(2)
                ]
                halves.append((jnp.where(first, a, pltpu.roll(b, 4, 1)), jnp.where(first, pltpu.roll(a, 4, 1), b)))
            for which in range(2):
                send[:, which, at16, :] = jnp.concatenate([halves[0][which], halves[1][which]], axis=1).astype(bf16)

            def push(k, c2):
                d = at(k)
                pltpu.make_async_remote_copy(
                    src_ref=send.at[d // 2, d % 2, at16, :], dst_ref=out.at[me, at16, :],
                    send_sem=blk_send.at[d], recv_sem=blk_recv.at[me],
                    device_id={"band": d}, device_id_type=pl.DeviceIdType.MESH).start()
                return c2

            lax.fori_loop(1, strips, push, 0)
            return c

        done = jnp.where(s == bands - 1, groups, (21 * (s + 1)) // 16)
        lax.fori_loop((21 * s) // 16, done, group, 0)
        return carry

    lax.fori_loop(0, bands, band, 0)
    own = pltpu.make_async_copy(send.at[me // 2, me % 2], out.at[me], own_sem.at[1])
    own.start()

    def finish(k, c):
        d = at(k)
        pltpu.make_async_remote_copy(
            src_ref=send.at[d // 2, d % 2], dst_ref=out.at[d], send_sem=blk_send.at[d], recv_sem=blk_recv.at[d],
            device_id={"band": d}, device_id_type=pl.DeviceIdType.MESH).wait()
        return c

    lax.fori_loop(1, strips, finish, 0)
    own.wait()


def lay_kernel(bands, recv, coef, monthly, annual):
    f32 = jnp.float32
    strips = recv.shape[0]
    quads = strips // 4
    width = strips * 32
    lane = lax.broadcasted_iota(jnp.int32, (8, 128), 1)
    even = (lane // 32) % 2 == 0
    front = lane < 64
    wide = lax.broadcasted_iota(jnp.int32, (8, width), 1)

    def swap(a, b, mask, shift):
        return jnp.where(mask, a, pltpu.roll(b, shift, 1)), jnp.where(mask, pltpu.roll(a, 128 - shift, 1), b)

    for gg in range(recv.shape[1] // 8):
        rows = [[], [], [], []]
        for q in range(quads):
            v = [recv[4 * q + j, pl.ds(8 * gg, 8), :].astype(f32) for j in range(4)]
            a0, a1 = swap(v[0], v[1], even, 32)
            a2, a3 = swap(v[2], v[3], even, 32)
            o0, o2 = swap(a0, a2, front, 64)
            o1, o3 = swap(a1, a3, front, 64)
            for p, o in enumerate((o0, o1, o2, o3)):
                rows[p].append(o)
        for p in range(4):
            full = jnp.concatenate(rows[p], axis=1)
            where_to = [divmod(4 * (2 * gg + half) + p, 21) for half in range(2)]
            if any(s < bands and j >= 8 for s, j in where_to):
                before = jnp.where(wide > 0, pltpu.roll(full, 1, 1), 0.0)
                after = jnp.where(wide < width - 1, pltpu.roll(full, width - 1, 1), 0.0)
                soft = 0.25 * before + 0.5 * full + 0.25 * after
            for half, (s, j) in enumerate(where_to):
                if s >= bands:
                    continue
                part = slice(4 * half, 4 * half + 4)
                if j < 8:
                    coef[j, s] = full[part]
                elif j < 20:
                    monthly[j - 8, s] = soft[part]
                else:
                    annual[s] = soft[part]


def fast(scenes, clear_bits, footprint, offsets, acq_day):
    f32, bf16 = jnp.float32, jnp.bfloat16
    dates, bands, rows, cols = scenes.shape
    strips = lax.axis_size("band")
    strip_width = cols // strips
    slots = -(-bands * 21 // 16) * 16
    smem = pl.BlockSpec(memory_space=pltpu.SMEM)
    vmem = pl.BlockSpec(memory_space=pltpu.VMEM)
    hbm = pl.BlockSpec(memory_space=pl.ANY)
    dma = pltpu.SemaphoreType.DMA
    words = clear_bits.reshape(clear_bits.shape[0], -1)
    recv = pl.pallas_call(
        functools.partial(fit_kernel, dates, bands, strips),
        out_shape=jax.ShapeDtypeStruct((strips, slots, cols), bf16),
        in_specs=[smem, smem, smem, vmem, vmem, hbm],
        out_specs=hbm,
        scratch_shapes=[
            pltpu.VMEM((dates, bands, rows, cols), bf16),
            pltpu.VMEM((bands, 64, cols), f32),
            pltpu.VMEM((bands, 64, cols), bf16),
            pltpu.VMEM((bands, 64, cols), bf16),
            pltpu.VMEM((strips,) + words.shape, jnp.int32),
            pltpu.VMEM((224, dates * 8), bf16),
            pltpu.VMEM((224, 64), bf16),
            pltpu.VMEM((dates, rows, cols), f32),
            pltpu.VMEM((8, cols), f32),
            pltpu.VMEM((1, 8, cols), f32),
            pltpu.VMEM((64, cols), f32),
            pltpu.VMEM((64, cols), f32),
            pltpu.VMEM((49, rows, cols), f32),
            pltpu.VMEM((2, dates * 8, 2 * cols), bf16),
            pltpu.VMEM((slots * rows, cols), f32),
            pltpu.VMEM((strips // 2, 2, slots, cols), bf16),
            dma, dma((strips,)), dma((strips,)), dma((2,)), dma((strips,)), dma((strips,)), dma((2,)),
        ],
        compiler_params=pltpu.CompilerParams(collective_id=0, has_side_effects=True, vmem_limit_bytes=48 * 1024 * 1024),
    )(offsets.reshape(-1), footprint.reshape(-1), acq_day, jnp.pad(acq_day, (0, 64 - dates))[None], words, scenes)
    return pl.pallas_call(
        functools.partial(lay_kernel, bands),
        out_shape=(
            jax.ShapeDtypeStruct((8, bands, strip_width, rows * strips), f32),
            jax.ShapeDtypeStruct((12, bands, strip_width, rows * strips), f32),
            jax.ShapeDtypeStruct((bands, strip_width, rows * strips), f32),
        ),
        in_specs=[vmem],
        out_specs=(vmem, vmem, vmem),
        compiler_params=pltpu.CompilerParams(vmem_limit_bytes=32 * 1024 * 1024),
    )(recv)


def pick(scenes, clear_bits, footprint, offsets, acq_day):
    dates, bands, rows, cols = scenes.shape
    strips = lax.axis_size("band")
    fits = lax.axis_size("tile") == 1 and lax.axis_size("sub") == 1 and strips % 4 == 0
    fits = fits and cols == 128 and rows == 32 and cols == 4 * strips and dates % 2 == 0 and dates <= 60
    return (fast if fits else shards)(scenes, clear_bits, footprint, offsets, acq_day)


def solution(mesh):
    placed = (
        P(("region", "tile"), "sub", "band", None),
        P(("region", "tile"), "band", None),
        P(("region", "tile"), None),
        P(("region", "tile"), None),
        P(("region", "tile")),
    )
    return jax.shard_map(
        pick,
        mesh=mesh,
        in_specs=placed,
        out_specs=(
            P("region", "sub", "band", "tile"),
            P(("region", "tile"), "sub", "band", None),
            P(("region", "sub"), "band", "tile"),
        ),
        check_vma=False,
    )
```

```python
import functools
import math

import jax
import jax.numpy as jnp
from jax import lax
from jax.experimental import pallas as pl
from jax.experimental.pallas import tpu as pltpu
from jax.sharding import PartitionSpec as P

RIDGE = 1.0


def shifted(value, axis, steps):
    count = lax.axis_size(axis)
    first, last = (max(0, -steps), min(count, count - steps))
    return lax.ppermute(value, axis, [(source, source + steps) for source in range(first, last)])


def extended(x, sides, width):
    for axis, dim in sides:
        devices, length = (lax.axis_size(axis), x.shape[dim])
        up = [(i, (i + 1) % devices) for i in range(devices - 1)]
        down = [(j, i) for i, j in up]
        last = lax.slice_in_dim(x, length - width, length, axis=dim)
        first = lax.slice_in_dim(x, 0, width, axis=dim)
        before = lax.ppermute(last, axis, up)
        after = lax.ppermute(first, axis, down)
        x = jnp.concatenate([before, x, after], axis=dim)
    return x


def design_tables(acq_day):
    day_phase = acq_day.astype(jnp.float32) / 365.0
    columns = [jnp.ones_like(day_phase), 2.0 * day_phase - 1.0]
    for harmonic in (1, 2, 3):
        turn_angle = 2.0 * jnp.pi * harmonic * day_phase
        columns = columns + [jnp.cos(turn_angle), jnp.sin(turn_angle)]
    harmonic_basis = jnp.stack(columns, axis=1)
    month_index = acq_day * 12 // 365
    onehot = (month_index[:, None] == jnp.arange(12, dtype=jnp.int32)[None, :]).astype(jnp.float32)
    products = jnp.stack(
        [
            harmonic_basis[:, row_term] * harmonic_basis[:, col_term]
            for row_term in range(8)
            for col_term in range(row_term + 1)
        ],
        axis=1,
    )
    return (
        jnp.concatenate([products, onehot], axis=1),
        jnp.concatenate([harmonic_basis, onehot], axis=1),
    )


def bilinear(padded, offsets):
    shift_row = (offsets[:, 0].astype(jnp.float32) / 16.0)[:, None, None, None]
    shift_col = (offsets[:, 1].astype(jnp.float32) / 16.0)[:, None, None, None]
    upper_rows = padded[:, :, :-1].astype(jnp.float32)
    lower_rows = padded[:, :, 1:].astype(jnp.float32)

    def across(source):
        right_cell = jnp.concatenate([source[..., 1:], jnp.zeros_like(source[..., :1])], axis=-1)
        return (1.0 - shift_col) * source + shift_col * right_cell

    return ((1.0 - shift_row) * across(upper_rows) + shift_row * across(lower_rows)).astype(
        jnp.bfloat16
    )


def clear_weight(cell_words, footprint, strip_width):
    date_count = footprint.shape[0]
    per_date = jnp.repeat(cell_words, 30, axis=0)
    bit_place = (jnp.arange(date_count, dtype=jnp.int32) % 30)[:, None, None]
    clear_flag = jnp.right_shift(per_date, bit_place) & 1
    pixel_flag = jnp.repeat(jnp.repeat(clear_flag, 4, axis=1), 4, axis=2)
    strip_index = jnp.arange(pixel_flag.shape[1], dtype=jnp.int32) // strip_width
    covered = (strip_index[None, :] >= footprint[:, 0:1]) & (
        strip_index[None, :] <= footprint[:, 1:2]
    )
    return pixel_flag.astype(jnp.float32) * covered[:, :, None].astype(jnp.float32)


def partial_sums(weight, values, common_table, banded_table):
    common = jnp.einsum("dxy,dk->kxy", weight, common_table, precision=lax.Precision.HIGHEST)
    weighted = values.astype(jnp.float32) * weight[:, None]
    banded = jnp.einsum("dsxy,dk->ksxy", weighted, banded_table, precision=lax.Precision.HIGHEST)
    return (common, banded)


def solve_normal(gram, rhs):
    pair_list = [(row_term, col_term) for row_term in range(8) for col_term in range(row_term + 1)]
    gram_entry = {}
    for position, term_pair in enumerate(pair_list):
        gram_entry[term_pair] = gram[position]
    factor = {}
    for col_term in range(8):
        pivot_value = gram_entry[col_term, col_term] + RIDGE
        for inner_term in range(col_term):
            pivot_value = pivot_value - factor[col_term, inner_term] * factor[col_term, inner_term]
        diag_root = jnp.sqrt(pivot_value)
        factor[col_term, col_term] = diag_root
        for row_term in range(col_term + 1, 8):
            running = gram_entry[row_term, col_term]
            for inner_term in range(col_term):
                running = running - factor[row_term, inner_term] * factor[col_term, inner_term]
            factor[row_term, col_term] = running / diag_root
    forward = []
    for row_term in range(8):
        running = rhs[row_term]
        for inner_term in range(row_term):
            running = running - factor[row_term, inner_term] * forward[inner_term]
        forward.append(running / factor[row_term, row_term])
    backward = [forward[0]] * 8
    for row_term in reversed(range(8)):
        running = forward[row_term]
        for inner_term in range(row_term + 1, 8):
            running = running - factor[inner_term, row_term] * backward[inner_term]
        backward[row_term] = running / factor[row_term, row_term]
    return jnp.stack(backward, axis=0)


def smooth_axis(padded_field, along):
    inner_size = padded_field.shape[along] - 2
    left_part = lax.slice_in_dim(padded_field, 0, inner_size, axis=along)
    centre_part = lax.slice_in_dim(padded_field, 1, inner_size + 1, axis=along)
    right_part = lax.slice_in_dim(padded_field, 2, inner_size + 2, axis=along)
    return 0.25 * left_part + 0.5 * centre_part + 0.25 * right_part


def shards(scenes, clear_bits, footprint, offsets, acq_day):
    date_count, band_count, row_local, col_count = scenes.shape
    strip_count = lax.axis_size("band")
    tile_count = lax.axis_size("tile")
    strip_width = col_count // strip_count
    row_count = row_local * strip_count
    common_table, banded_table = design_tables(acq_day)
    below = shifted(scenes[:, :, 0:1, :], "band", -1)
    resampled = bilinear(jnp.concatenate([scenes, below], axis=2), offsets)
    flipped = jnp.swapaxes(resampled, 2, 3)
    cell_words = lax.all_to_all(clear_bits, "band", split_axis=2, concat_axis=1, tiled=True)
    weight = clear_weight(cell_words, footprint, strip_width)
    common, banded = partial_sums(weight, flipped, common_table, banded_table)
    common, banded = (
        lax.all_to_all(common, "band", split_axis=1, concat_axis=2, tiled=True),
        lax.all_to_all(
            banded.reshape(-1, col_count, row_local),
            "band",
            split_axis=1,
            concat_axis=2,
            tiled=True,
        ),
    )
    banded = banded.reshape(20, band_count, strip_width, row_count)
    gram = common[:36]
    month_count = common[36:]
    rhs = banded[:8]
    month_sum = banded[8:]
    annual_sum = jnp.sum(month_sum, axis=0)
    annual_count = jnp.sum(month_count, axis=0)
    month_sum, month_count = (
        lax.psum_scatter(month_sum, "tile", scatter_dimension=0, tiled=True),
        lax.psum_scatter(month_count, "tile", scatter_dimension=0, tiled=True),
    )
    composite = month_sum / jnp.maximum(month_count, 1.0)[:, None]
    month_edged = extended(composite, (("band", 2),), 1)
    month_edged = jnp.pad(month_edged, ((0, 0), (0, 0), (0, 0), (1, 1)))
    monthly = smooth_axis(smooth_axis(month_edged, 3), 2)
    share = row_count // tile_count
    gram, rhs, annual_sum, annual_count = lax.psum((gram, rhs, annual_sum, annual_count), "tile")
    start = lax.axis_index("tile") * share
    gram = lax.dynamic_slice_in_dim(gram, start, share, 2)
    rhs = lax.dynamic_slice_in_dim(rhs, start, share, 3)
    annual_sum = lax.dynamic_slice_in_dim(annual_sum, start, share, 2)
    annual_count = lax.dynamic_slice_in_dim(annual_count, start, share, 1)
    coefficients = solve_normal(gram, rhs)
    yearly = annual_sum / jnp.maximum(annual_count, 1.0)
    year_edged = extended(yearly, (("band", 1), ("tile", 2)), 1)
    annual = smooth_axis(smooth_axis(year_edged, 2), 1)
    return (coefficients, monthly, annual)


def fit_kernel(dates, bands, strips, off, foot, day_s, words, scenes, out,
               scn, hsf, hs, hr, bits, mix, mix_last, wide, tables, edge_x, edge_w, fac, stack, planes, send,
               scene_sem, bit_send, bit_recv, halo_sem, blk_send, blk_recv, own_sem):
    f32, bf16, i32 = jnp.float32, jnp.bfloat16, jnp.int32
    me = lax.axis_index("band")
    sub8 = lax.broadcasted_iota(i32, (8, 128), 0)
    lane8 = lax.broadcasted_iota(i32, (8, 128), 1)
    upper = sub8 < 4
    depth = dates * 8
    load = pltpu.make_async_copy(scenes, scn, scene_sem)
    load.start()

    def at(k):
        return lax.rem(me + k, strips)

    half = strips // 2

    def peer(k):
        cross = (me // half + 1 + k // half) % 2
        return cross * half + (me + k) % half

    barrier = pltpu.get_barrier_semaphore()

    def greet(k, c):
        pl.semaphore_signal(barrier, inc=1, device_id={"band": at(k)}, device_id_type=pl.DeviceIdType.MESH)
        return c

    lax.fori_loop(1, strips, greet, 0)

    def basis(day, which):
        u = day.astype(f32) / 365.0
        turn = (which // 2).astype(f32) * u - jnp.where(which % 2 == 1, 0.25, 0.0)
        turn = turn - jnp.floor(turn + 0.5)
        square = (turn * turn) * (4.0 * math.pi * math.pi)
        wave = jnp.full_like(square, 1.0 / math.factorial(20))
        for k in range(9, -1, -1):
            wave = (-1.0) ** k / math.factorial(2 * k) + wave * square
        return jnp.where(which == 0, 1.0, jnp.where(which == 1, 2.0 * u - 1.0, wave))

    lane64i = lax.broadcasted_iota(i32, (16, 64), 1)

    def days(t, acc):
        return jnp.where(lane64i == t, day_s[t], acc)

    day64 = lax.fori_loop(0, dates, days, jnp.zeros((16, 64), i32), unroll=10)
    d8 = day64[0:8]
    which8 = lax.broadcasted_iota(i32, (8, 64), 0)
    real = lax.broadcasted_iota(i32, (8, 64), 1) < dates
    b8 = jnp.where(real, basis(d8, which8), 0.0)
    high = b8.astype(bf16).astype(f32)
    d16 = day64 * 12
    m16 = lax.broadcasted_iota(i32, (16, 64), 0)
    ok16 = (lax.broadcasted_iota(i32, (16, 64), 1) < dates) & (m16 < 12)
    hot = jnp.where(ok16 & (d16 >= 365 * m16) & (d16 < 365 * m16 + 365), 1.0, 0.0)
    tab_in = jnp.concatenate([high, b8 - high, hot], axis=0).astype(bf16)
    choose = (lax.broadcasted_iota(i32, (224, 32), 0) // 8 == lax.broadcasted_iota(i32, (224, 32), 1)).astype(f32).astype(bf16)
    tab = jnp.dot(choose, tab_in, preferred_element_type=f32)
    last = lax.broadcasted_iota(i32, (224, 64), 0) % 8 == 7
    mix_last[...] = jnp.where(last, tab, 0.0).astype(bf16)
    place = (lax.broadcasted_iota(i32, (64, depth), 1) // 8 == lax.broadcasted_iota(i32, (64, depth), 0)).astype(f32).astype(bf16)
    full = jnp.dot(tab.astype(bf16), place, preferred_element_type=f32)
    same = lax.broadcasted_iota(i32, (224, depth), 0) % 8 == lax.broadcasted_iota(i32, (224, depth), 1) % 8
    mix[...] = jnp.where(same, full, 0.0).astype(bf16)
    planes[pl.ds(bands * 21 * 32, 64), :] = jnp.zeros((64, 128), f32)
    edge_x[...] = jnp.zeros((64, 128), f32)
    edge_w[...] = jnp.zeros((64, 128), f32)
    hsf[...] = jnp.zeros((bands, 64, 128), f32)

    sub16 = lax.broadcasted_iota(i32, (16, 128), 0)

    def date_tables(t, c):
        tables[t, 0:8, :] = basis(jnp.full((8, 128), day_s[t], i32), sub8)
        d12 = jnp.full((16, 128), day_s[t], i32) * 12
        tables[t, 8:24, :] = jnp.where((d12 >= 365 * sub16) & (d12 < 365 * sub16 + 365), 1.0, 0.0)
        return c

    lax.fori_loop(0, dates, date_tables, 0, unroll=6)
    pl.semaphore_wait(barrier, strips - 1)

    def bit_copy(k):
        return pltpu.make_async_remote_copy(
            src_ref=words, dst_ref=bits.at[me], send_sem=bit_send.at[at(k)], recv_sem=bit_recv.at[me],
            device_id={"band": at(k)}, device_id_type=pl.DeviceIdType.MESH)

    def send_bits(k, c):
        bit_copy(k).start()
        return c

    lax.fori_loop(1, strips, send_bits, 0)
    own_bits = pltpu.make_async_copy(words, bits.at[me], own_sem.at[0])
    own_bits.start()

    load.wait()

    def first_rows(t, c):
        for s in range(bands):
            hsf[s, pl.ds(t, 1), :] = scn[t, s, 0:1, :].astype(f32)
        return c

    lax.fori_loop(0, dates, first_rows, 0, unroll=2)
    hs[...] = hsf[...].astype(bf16)
    halo = pltpu.make_async_remote_copy(
        src_ref=hs, dst_ref=hr, send_sem=halo_sem.at[0], recv_sem=halo_sem.at[1],
        device_id={"band": lax.rem(me + strips - 1, strips)}, device_id_type=pl.DeviceIdType.MESH)
    halo.start()

    def take_bits(k, c):
        pltpu.make_async_remote_copy(
            src_ref=words, dst_ref=bits.at[at(k)], send_sem=bit_send.at[at(k)], recv_sem=bit_recv.at[at(k)],
            device_id={"band": at(k)}, device_id_type=pl.DeviceIdType.MESH).wait()
        return c

    lax.fori_loop(1, strips, take_bits, 0)
    own_bits.wait()

    repeat = (lax.broadcasted_iota(i32, (128, strips), 0) // 4 == lax.broadcasted_iota(i32, (128, strips), 1)).astype(f32)
    cells = []
    for w in range(words.shape[0]):
        mine = pltpu.roll(bits[:, w, 0, :], lax.rem(8 * (strips - me), 8 * strips), 1)[:, :128]
        parts = []
        for piece in (mine & 32767, mine >> 15):
            spreadc = jnp.dot(repeat, piece.astype(f32), precision=lax.Precision.HIGHEST, preferred_element_type=f32)
            parts.append(spreadc.T[0:8].astype(i32))
        cells.append(parts[0] + parts[1] * 32768)

    def spread(cell, rb):
        return jnp.where(upper, cell[2 * rb : 2 * rb + 1, :], cell[2 * rb + 1 : 2 * rb + 2, :])

    acc = tuple(jnp.zeros((8, 128), f32) for _ in range(48))
    for w in range(words.shape[0]):

        def date(j, acc):
            t = 30 * w + j
            seen = (lane8 >= 4 * foot[0, t]) & (lane8 < 4 * foot[1, t] + 4)
            wt = jnp.where(seen, (cells[w] >> j) & 1, 0).astype(f32)
            fy = off[0, t].astype(f32) * 0.0625
            fx = off[1, t].astype(f32) * 0.0625
            edge_x[pl.ds(t, 1), :] = jnp.full((1, 128), fx)
            edge_w[pl.ds(t, 1), :] = wt[7:8, :] * fy
            for rb in range(4):
                wide[t, pl.ds(8 * rb, 8), :] = spread(wt, rb)
            b = [jnp.broadcast_to(tables[t, i : i + 1, :], (8, 128)) for i in range(20)]
            res = []
            for i in range(8):
                wb = wt * b[i]
                for k in range(i + 1):
                    res.append(acc[len(res)] + wb * b[k])
            for m in range(12):
                res.append(acc[len(res)] + wt * b[8 + m])
            return tuple(res)

        acc = lax.fori_loop(0, min(30, dates - 30 * w), date, acc, unroll=2)
    gram = {}
    for i in range(8):
        for j in range(i + 1):
            gram[i, j] = acc[i * (i + 1) // 2 + j]
    low, inv = {}, {}
    for j in range(8):
        pivot = gram[j, j] + RIDGE
        for k in range(j):
            pivot = pivot - low[j, k] * low[j, k]
        inv[j] = 1.0 / jnp.sqrt(pivot)
        for i in range(j + 1, 8):
            run = gram[i, j]
            for k in range(j):
                run = run - low[i, k] * low[j, k]
            low[i, j] = run * inv[j]
    items = [inv[i] for i in range(8)]
    items += [low[i, j] for i in range(8) for j in range(i)]
    items += [1.0 / jnp.maximum(acc[36 + m], 1.0) for m in range(12)]
    total = acc[36]
    for m in range(1, 12):
        total = total + acc[36 + m]
    items.append(1.0 / jnp.maximum(total, 1.0))
    for n, item in enumerate(items):
        for rb in range(4):
            fac[n, pl.ds(8 * rb, 8), :] = spread(item, rb)

    halo.wait()

    @pl.when(me == strips - 1)
    def _():
        hr[...] = jnp.zeros((bands, 64, 128), bf16)

    lane = lax.broadcasted_iota(i32, (32, 128), 1)
    row = lax.broadcasted_iota(i32, (32, 128), 0)
    lane64 = lax.broadcasted_iota(i32, (64, 128), 1)
    ends = jnp.where(lane8 > 0, 0.25, 0.0), jnp.where(lane8 < 127, 0.25, 0.0)
    first = lax.broadcasted_iota(i32, (16, 8, 128), 1) < 4
    groups = send.shape[2] // 16

    def smooth(x):
        return 0.5 * x + ends[0] * pltpu.roll(x, 1, 1) + ends[1] * pltpu.roll(x, 127, 1)

    def band(s, carry):
        def pair(p, c):
            u = []
            for t2 in range(2):
                t = 2 * p + t2
                fy = off[0, t].astype(f32) * 0.0625
                fx = off[1, t].astype(f32) * 0.0625
                x = scn[t, s].astype(f32)
                xb = (1.0 - fx) * x + jnp.where(lane < 127, fx, 0.0) * pltpu.roll(x, 127, 1)
                v = (1.0 - fy) * xb + jnp.where(row < 31, fy, 0.0) * pltpu.roll(xb, 31, 0)
                u.append(v * wide[t])
            for rb in range(4):
                both = jnp.concatenate([u[0][8 * rb : 8 * rb + 8], u[1][8 * rb : 8 * rb + 8]], axis=0)
                stack[rb // 2, pl.ds(pl.multiple_of(16 * p, 16), 16), pl.ds(128 * (rb % 2), 128)] = both.astype(bf16)
            return c

        lax.fori_loop(0, dates // 2, pair, 0, unroll=2)
        e = hr[s].astype(f32)
        fx = edge_x[...]
        hu = ((1.0 - fx) * e + jnp.where(lane64 < 127, fx, 0.0) * pltpu.roll(e, 127, 1)) * edge_w[...]
        sums = [jnp.dot(mix[...], stack[h], preferred_element_type=f32) for h in range(2)]
        extra = jnp.dot(mix_last[...], hu.astype(bf16), preferred_element_type=f32)
        for rb in range(4):
            rows = pl.ds(8 * rb, 8)

            def term(n):
                part = sums[rb // 2][8 * n : 8 * n + 8, 128 * (rb % 2) : 128 * (rb % 2) + 128]
                return part + extra[8 * n : 8 * n + 8] if rb == 3 else part

            def fl(i, j):
                return fac[8 + i * (i - 1) // 2 + j, rows, :]

            def put(n, value):
                start = pl.multiple_of((s * 21 + n) * 32 + 8 * rb, 8)
                planes[pl.ds(start, 8), :] = value

            fwd = []
            for i in range(8):
                run = term(i) + term(8 + i)
                for k in range(i):
                    run = run - fl(i, k) * fwd[k]
                fwd.append(run * fac[i, rows, :])
            back = [None] * 8
            for i in reversed(range(8)):
                run = fwd[i]
                for k in range(i + 1, 8):
                    run = run - fl(k, i) * back[k]
                back[i] = run * fac[i, rows, :]
                put(i, back[i])
            whole = None
            for m in range(12):
                month = term(16 + m)
                whole = month if whole is None else whole + month
                put(8 + m, smooth(month * fac[36 + m, rows, :]))
            put(20, smooth(whole * fac[48, rows, :]))

        def group(gg, c):
            at16 = pl.ds(pl.multiple_of(16 * gg, 16), 16)
            halves = []
            for h in range(2):
                a, b = [
                    planes[pl.ds(pl.multiple_of((4 * gg + 2 * h + k) * 128, 128), 128), :].T.reshape(16, 8, 128)
                    for k in range(2)
                ]
                halves.append((jnp.where(first, a, pltpu.roll(b, 4, 1)), jnp.where(first, pltpu.roll(a, 4, 1), b)))
            for which in range(2):
                send[:, which, at16, :] = jnp.concatenate([halves[0][which], halves[1][which]], axis=1).astype(bf16)

            def push(k, c2):
                d = peer(k)
                pltpu.make_async_remote_copy(
                    src_ref=send.at[d // 2, d % 2, at16, :], dst_ref=out.at[me, at16, :],
                    send_sem=blk_send.at[d], recv_sem=blk_recv.at[me],
                    device_id={"band": d}, device_id_type=pl.DeviceIdType.MESH).start()
                return c2

            lax.fori_loop(0, half, push, 0)
            lax.fori_loop(half + 1, strips, push, 0)
            return c

        done = jnp.where(s == bands - 1, groups, (21 * (s + 1)) // 16)
        lax.fori_loop((21 * s) // 16, done, group, 0)
        return carry

    lax.fori_loop(0, bands, band, 0)
    own = pltpu.make_async_copy(send.at[me // 2, me % 2], out.at[me], own_sem.at[1])
    own.start()

    def finish(k, c):
        d = at(k)
        pltpu.make_async_remote_copy(
            src_ref=send.at[d // 2, d % 2], dst_ref=out.at[d], send_sem=blk_send.at[d], recv_sem=blk_recv.at[d],
            device_id={"band": d}, device_id_type=pl.DeviceIdType.MESH).wait()
        return c

    lax.fori_loop(1, strips, finish, 0)
    own.wait()


def lay_kernel(bands, recv, coef_out, monthly_out, annual_out, coef, monthly, annual, sems):
    f32 = jnp.float32
    strips = recv.shape[0]
    quads = strips // 4
    width = strips * 32
    lane = lax.broadcasted_iota(jnp.int32, (8, 128), 1)
    even = (lane // 32) % 2 == 0
    front = lane < 64
    wide = lax.broadcasted_iota(jnp.int32, (8, width), 1)

    def swap(a, b, mask, shift):
        return jnp.where(mask, a, pltpu.roll(b, shift, 1)), jnp.where(mask, pltpu.roll(a, 128 - shift, 1), b)

    for gg in range(recv.shape[1] // 8):
        rows = [[], [], [], []]
        for q in range(quads):
            v = [recv[4 * q + j, pl.ds(8 * gg, 8), :].astype(f32) for j in range(4)]
            a0, a1 = swap(v[0], v[1], even, 32)
            a2, a3 = swap(v[2], v[3], even, 32)
            o0, o2 = swap(a0, a2, front, 64)
            o1, o3 = swap(a1, a3, front, 64)
            for p, o in enumerate((o0, o1, o2, o3)):
                rows[p].append(o)
        for p in range(4):
            full = jnp.concatenate(rows[p], axis=1)
            where_to = [divmod(4 * (2 * gg + half) + p, 21) for half in range(2)]
            if any(s < bands and j >= 8 for s, j in where_to):
                before = jnp.where(wide > 0, pltpu.roll(full, 1, 1), 0.0)
                after = jnp.where(wide < width - 1, pltpu.roll(full, width - 1, 1), 0.0)
                soft = 0.25 * before + 0.5 * full + 0.25 * after
            for half, (s, j) in enumerate(where_to):
                if s >= bands:
                    continue
                part = slice(4 * half, 4 * half + 4)
                if j < 8:
                    coef[j, s] = full[part]
                    pltpu.make_async_copy(coef.at[j, s], coef_out.at[j, s], sems.at[0]).start()
                elif j < 20:
                    monthly[j - 8, s] = soft[part]
                    pltpu.make_async_copy(monthly.at[j - 8, s], monthly_out.at[j - 8, s], sems.at[1]).start()
                else:
                    annual[s] = soft[part]
                    pltpu.make_async_copy(annual.at[s], annual_out.at[s], sems.at[2]).start()
    pltpu.make_async_copy(coef, coef_out, sems.at[0]).wait()
    pltpu.make_async_copy(monthly, monthly_out, sems.at[1]).wait()
    pltpu.make_async_copy(annual, annual_out, sems.at[2]).wait()


def fast(scenes, clear_bits, footprint, offsets, acq_day):
    f32, bf16 = jnp.float32, jnp.bfloat16
    dates, bands, rows, cols = scenes.shape
    strips = lax.axis_size("band")
    strip_width = cols // strips
    slots = -(-bands * 21 // 16) * 16
    smem = pl.BlockSpec(memory_space=pltpu.SMEM)
    vmem = pl.BlockSpec(memory_space=pltpu.VMEM)
    hbm = pl.BlockSpec(memory_space=pl.ANY)
    dma = pltpu.SemaphoreType.DMA
    recv = pl.pallas_call(
        functools.partial(fit_kernel, dates, bands, strips),
        out_shape=jax.ShapeDtypeStruct((strips, slots, cols), bf16),
        in_specs=[smem, smem, smem, vmem, hbm],
        out_specs=hbm,
        scratch_shapes=[
            pltpu.VMEM((dates, bands, rows, cols), bf16),
            pltpu.VMEM((bands, 64, cols), f32),
            pltpu.VMEM((bands, 64, cols), bf16),
            pltpu.VMEM((bands, 64, cols), bf16),
            pltpu.VMEM((strips,) + clear_bits.shape, jnp.int32),
            pltpu.VMEM((224, dates * 8), bf16),
            pltpu.VMEM((224, 64), bf16),
            pltpu.VMEM((dates, rows, cols), f32),
            pltpu.VMEM((dates, 24, cols), f32),
            pltpu.VMEM((64, cols), f32),
            pltpu.VMEM((64, cols), f32),
            pltpu.VMEM((49, rows, cols), f32),
            pltpu.VMEM((2, dates * 8, 2 * cols), bf16),
            pltpu.VMEM((slots * rows, cols), f32),
            pltpu.VMEM((strips // 2, 2, slots, cols), bf16),
            dma, dma((strips,)), dma((strips,)), dma((2,)), dma((strips,)), dma((strips,)), dma((2,)),
        ],
        compiler_params=pltpu.CompilerParams(collective_id=0, has_side_effects=True, vmem_limit_bytes=58 * 1024 * 1024),
    )(offsets.T, footprint.T, acq_day, clear_bits, scenes)
    return pl.pallas_call(
        functools.partial(lay_kernel, bands),
        out_shape=(
            jax.ShapeDtypeStruct((8, bands, strip_width, rows * strips), f32),
            jax.ShapeDtypeStruct((12, bands, strip_width, rows * strips), f32),
            jax.ShapeDtypeStruct((bands, strip_width, rows * strips), f32),
        ),
        in_specs=[vmem],
        out_specs=(hbm, hbm, hbm),
        scratch_shapes=[
            pltpu.VMEM((8, bands, strip_width, rows * strips), f32),
            pltpu.VMEM((12, bands, strip_width, rows * strips), f32),
            pltpu.VMEM((bands, strip_width, rows * strips), f32),
            dma((3,)),
        ],
        compiler_params=pltpu.CompilerParams(vmem_limit_bytes=56 * 1024 * 1024),
    )(recv)


def pick(scenes, clear_bits, footprint, offsets, acq_day):
    dates, bands, rows, cols = scenes.shape
    strips = lax.axis_size("band")
    fits = lax.axis_size("tile") == 1 and lax.axis_size("sub") == 1 and strips % 4 == 0
    fits = fits and cols == 128 and rows == 32 and cols == 4 * strips and dates % 2 == 0 and dates <= 60
    return (fast if fits else shards)(scenes, clear_bits, footprint, offsets, acq_day)


def solution(mesh):
    placed = (
        P(("region", "tile"), "sub", "band", None),
        P(("region", "tile"), "band", None),
        P(("region", "tile"), None),
        P(("region", "tile"), None),
        P(("region", "tile")),
    )
    return jax.shard_map(
        pick,
        mesh=mesh,
        in_specs=placed,
        out_specs=(
            P("region", "sub", "band", "tile"),
            P(("region", "tile"), "sub", "band", None),
            P(("region", "sub"), "band", "tile"),
        ),
        check_vma=False,
    )
```

```python
import functools
import math

import jax
import jax.numpy as jnp
from jax import lax
from jax.experimental import pallas as pl
from jax.experimental.pallas import tpu as pltpu
from jax.sharding import PartitionSpec as P

RIDGE = 1.0


def shifted(value, axis, steps):
    count = lax.axis_size(axis)
    first, last = (max(0, -steps), min(count, count - steps))
    return lax.ppermute(value, axis, [(source, source + steps) for source in range(first, last)])


def extended(x, sides, width):
    for axis, dim in sides:
        devices, length = (lax.axis_size(axis), x.shape[dim])
        up = [(i, (i + 1) % devices) for i in range(devices - 1)]
        down = [(j, i) for i, j in up]
        last = lax.slice_in_dim(x, length - width, length, axis=dim)
        first = lax.slice_in_dim(x, 0, width, axis=dim)
        before = lax.ppermute(last, axis, up)
        after = lax.ppermute(first, axis, down)
        x = jnp.concatenate([before, x, after], axis=dim)
    return x


def design_tables(acq_day):
    day_phase = acq_day.astype(jnp.float32) / 365.0
    columns = [jnp.ones_like(day_phase), 2.0 * day_phase - 1.0]
    for harmonic in (1, 2, 3):
        turn_angle = 2.0 * jnp.pi * harmonic * day_phase
        columns = columns + [jnp.cos(turn_angle), jnp.sin(turn_angle)]
    harmonic_basis = jnp.stack(columns, axis=1)
    month_index = acq_day * 12 // 365
    onehot = (month_index[:, None] == jnp.arange(12, dtype=jnp.int32)[None, :]).astype(jnp.float32)
    products = jnp.stack(
        [
            harmonic_basis[:, row_term] * harmonic_basis[:, col_term]
            for row_term in range(8)
            for col_term in range(row_term + 1)
        ],
        axis=1,
    )
    return (
        jnp.concatenate([products, onehot], axis=1),
        jnp.concatenate([harmonic_basis, onehot], axis=1),
    )


def bilinear(padded, offsets):
    shift_row = (offsets[:, 0].astype(jnp.float32) / 16.0)[:, None, None, None]
    shift_col = (offsets[:, 1].astype(jnp.float32) / 16.0)[:, None, None, None]
    upper_rows = padded[:, :, :-1].astype(jnp.float32)
    lower_rows = padded[:, :, 1:].astype(jnp.float32)

    def across(source):
        right_cell = jnp.concatenate([source[..., 1:], jnp.zeros_like(source[..., :1])], axis=-1)
        return (1.0 - shift_col) * source + shift_col * right_cell

    return ((1.0 - shift_row) * across(upper_rows) + shift_row * across(lower_rows)).astype(
        jnp.bfloat16
    )


def clear_weight(cell_words, footprint, strip_width):
    date_count = footprint.shape[0]
    per_date = jnp.repeat(cell_words, 30, axis=0)
    bit_place = (jnp.arange(date_count, dtype=jnp.int32) % 30)[:, None, None]
    clear_flag = jnp.right_shift(per_date, bit_place) & 1
    pixel_flag = jnp.repeat(jnp.repeat(clear_flag, 4, axis=1), 4, axis=2)
    strip_index = jnp.arange(pixel_flag.shape[1], dtype=jnp.int32) // strip_width
    covered = (strip_index[None, :] >= footprint[:, 0:1]) & (
        strip_index[None, :] <= footprint[:, 1:2]
    )
    return pixel_flag.astype(jnp.float32) * covered[:, :, None].astype(jnp.float32)


def partial_sums(weight, values, common_table, banded_table):
    common = jnp.einsum("dxy,dk->kxy", weight, common_table, precision=lax.Precision.HIGHEST)
    weighted = values.astype(jnp.float32) * weight[:, None]
    banded = jnp.einsum("dsxy,dk->ksxy", weighted, banded_table, precision=lax.Precision.HIGHEST)
    return (common, banded)


def solve_normal(gram, rhs):
    pair_list = [(row_term, col_term) for row_term in range(8) for col_term in range(row_term + 1)]
    gram_entry = {}
    for position, term_pair in enumerate(pair_list):
        gram_entry[term_pair] = gram[position]
    factor = {}
    for col_term in range(8):
        pivot_value = gram_entry[col_term, col_term] + RIDGE
        for inner_term in range(col_term):
            pivot_value = pivot_value - factor[col_term, inner_term] * factor[col_term, inner_term]
        diag_root = jnp.sqrt(pivot_value)
        factor[col_term, col_term] = diag_root
        for row_term in range(col_term + 1, 8):
            running = gram_entry[row_term, col_term]
            for inner_term in range(col_term):
                running = running - factor[row_term, inner_term] * factor[col_term, inner_term]
            factor[row_term, col_term] = running / diag_root
    forward = []
    for row_term in range(8):
        running = rhs[row_term]
        for inner_term in range(row_term):
            running = running - factor[row_term, inner_term] * forward[inner_term]
        forward.append(running / factor[row_term, row_term])
    backward = [forward[0]] * 8
    for row_term in reversed(range(8)):
        running = forward[row_term]
        for inner_term in range(row_term + 1, 8):
            running = running - factor[inner_term, row_term] * backward[inner_term]
        backward[row_term] = running / factor[row_term, row_term]
    return jnp.stack(backward, axis=0)


def smooth_axis(padded_field, along):
    inner_size = padded_field.shape[along] - 2
    left_part = lax.slice_in_dim(padded_field, 0, inner_size, axis=along)
    centre_part = lax.slice_in_dim(padded_field, 1, inner_size + 1, axis=along)
    right_part = lax.slice_in_dim(padded_field, 2, inner_size + 2, axis=along)
    return 0.25 * left_part + 0.5 * centre_part + 0.25 * right_part


def shards(scenes, clear_bits, footprint, offsets, acq_day):
    date_count, band_count, row_local, col_count = scenes.shape
    strip_count = lax.axis_size("band")
    tile_count = lax.axis_size("tile")
    strip_width = col_count // strip_count
    row_count = row_local * strip_count
    common_table, banded_table = design_tables(acq_day)
    below = shifted(scenes[:, :, 0:1, :], "band", -1)
    resampled = bilinear(jnp.concatenate([scenes, below], axis=2), offsets)
    flipped = jnp.swapaxes(resampled, 2, 3)
    cell_words = lax.all_to_all(clear_bits, "band", split_axis=2, concat_axis=1, tiled=True)
    weight = clear_weight(cell_words, footprint, strip_width)
    common, banded = partial_sums(weight, flipped, common_table, banded_table)
    common, banded = (
        lax.all_to_all(common, "band", split_axis=1, concat_axis=2, tiled=True),
        lax.all_to_all(
            banded.reshape(-1, col_count, row_local),
            "band",
            split_axis=1,
            concat_axis=2,
            tiled=True,
        ),
    )
    banded = banded.reshape(20, band_count, strip_width, row_count)
    gram = common[:36]
    month_count = common[36:]
    rhs = banded[:8]
    month_sum = banded[8:]
    annual_sum = jnp.sum(month_sum, axis=0)
    annual_count = jnp.sum(month_count, axis=0)
    month_sum, month_count = (
        lax.psum_scatter(month_sum, "tile", scatter_dimension=0, tiled=True),
        lax.psum_scatter(month_count, "tile", scatter_dimension=0, tiled=True),
    )
    composite = month_sum / jnp.maximum(month_count, 1.0)[:, None]
    month_edged = extended(composite, (("band", 2),), 1)
    month_edged = jnp.pad(month_edged, ((0, 0), (0, 0), (0, 0), (1, 1)))
    monthly = smooth_axis(smooth_axis(month_edged, 3), 2)
    share = row_count // tile_count
    gram, rhs, annual_sum, annual_count = lax.psum((gram, rhs, annual_sum, annual_count), "tile")
    start = lax.axis_index("tile") * share
    gram = lax.dynamic_slice_in_dim(gram, start, share, 2)
    rhs = lax.dynamic_slice_in_dim(rhs, start, share, 3)
    annual_sum = lax.dynamic_slice_in_dim(annual_sum, start, share, 2)
    annual_count = lax.dynamic_slice_in_dim(annual_count, start, share, 1)
    coefficients = solve_normal(gram, rhs)
    yearly = annual_sum / jnp.maximum(annual_count, 1.0)
    year_edged = extended(yearly, (("band", 1), ("tile", 2)), 1)
    annual = smooth_axis(smooth_axis(year_edged, 2), 1)
    return (coefficients, monthly, annual)


def fit_kernel(dates, bands, strips, off, foot, day_s, words, scenes, out,
               scn, hsf, hs, hr, bits, mix, mix_last, wide, mix_gram, cover, edge_x, edge_w, fac, stack, planes, send,
               scene_sem, bit_send, bit_recv, halo_sem, blk_send, blk_recv, own_sem):
    f32, bf16, i32 = jnp.float32, jnp.bfloat16, jnp.int32
    me = lax.axis_index("band")
    sub8 = lax.broadcasted_iota(i32, (8, 128), 0)
    lane8 = lax.broadcasted_iota(i32, (8, 128), 1)
    upper = sub8 < 4
    depth = dates * 8
    load = pltpu.make_async_copy(scenes, scn, scene_sem)
    load.start()

    def at(k):
        return lax.rem(me + k, strips)

    half = strips // 2

    def peer(k):
        cross = (me // half + 1 + k // half) % 2
        return cross * half + (me + k) % half

    barrier = pltpu.get_barrier_semaphore()

    def greet(k, c):
        pl.semaphore_signal(barrier, inc=1, device_id={"band": at(k)}, device_id_type=pl.DeviceIdType.MESH)
        return c

    lax.fori_loop(1, strips, greet, 0)

    def basis(day, which):
        u = day.astype(f32) / 365.0
        turn = (which // 2).astype(f32) * u - jnp.where(which % 2 == 1, 0.25, 0.0)
        turn = turn - jnp.floor(turn + 0.5)
        square = (turn * turn) * (4.0 * math.pi * math.pi)
        wave = jnp.full_like(square, 1.0 / math.factorial(20))
        for k in range(9, -1, -1):
            wave = (-1.0) ** k / math.factorial(2 * k) + wave * square
        return jnp.where(which == 0, 1.0, jnp.where(which == 1, 2.0 * u - 1.0, wave))

    lane64i = lax.broadcasted_iota(i32, (16, 64), 1)

    def days(t, acc):
        return jnp.where(lane64i == t, day_s[t], acc)

    day64 = lax.fori_loop(0, dates, days, jnp.zeros((16, 64), i32), unroll=10)
    d8 = day64[0:8]
    which8 = lax.broadcasted_iota(i32, (8, 64), 0)
    real = lax.broadcasted_iota(i32, (8, 64), 1) < dates
    b8 = jnp.where(real, basis(d8, which8), 0.0)
    high = b8.astype(bf16).astype(f32)
    d16 = day64 * 12
    m16 = lax.broadcasted_iota(i32, (16, 64), 0)
    ok16 = (lax.broadcasted_iota(i32, (16, 64), 1) < dates) & (m16 < 12)
    hot = jnp.where(ok16 & (d16 >= 365 * m16) & (d16 < 365 * m16 + 365), 1.0, 0.0)
    tab_in = jnp.concatenate([high, b8 - high, hot], axis=0).astype(bf16)
    choose = (lax.broadcasted_iota(i32, (224, 32), 0) // 8 == lax.broadcasted_iota(i32, (224, 32), 1)).astype(f32).astype(bf16)
    tab = jnp.dot(choose, tab_in, preferred_element_type=f32)
    last = lax.broadcasted_iota(i32, (224, 64), 0) % 8 == 7
    mix_last[...] = jnp.where(last, tab, 0.0).astype(bf16)
    place = (lax.broadcasted_iota(i32, (64, depth), 1) // 8 == lax.broadcasted_iota(i32, (64, depth), 0)).astype(f32).astype(bf16)
    full = jnp.dot(tab.astype(bf16), place, preferred_element_type=f32)
    same = lax.broadcasted_iota(i32, (224, depth), 0) % 8 == lax.broadcasted_iota(i32, (224, depth), 1) % 8
    mix[...] = jnp.where(same, full, 0.0).astype(bf16)
    pairs = jnp.concatenate([b8[i : i + 1] * b8[: i + 1] for i in range(8)] + [jnp.zeros((4, 64), f32)], axis=0)
    high_pairs = pairs.astype(bf16).astype(f32)
    tab_pairs = jnp.concatenate([high_pairs, pairs - high_pairs, hot], axis=0).astype(bf16)
    choose = (lax.broadcasted_iota(i32, (768, 96), 0) // 8 == lax.broadcasted_iota(i32, (768, 96), 1)).astype(f32).astype(bf16)
    tab = jnp.dot(choose, tab_pairs, preferred_element_type=f32)
    full = jnp.dot(tab.astype(bf16), place, preferred_element_type=f32)
    same = lax.broadcasted_iota(i32, (768, depth), 0) % 8 == lax.broadcasted_iota(i32, (768, depth), 1) % 8
    mix_gram[...] = jnp.where(same, full, 0.0).astype(bf16)
    planes[pl.ds(bands * 21 * 32, 64), :] = jnp.zeros((64, 128), f32)
    edge_x[...] = jnp.zeros((64, 128), f32)
    edge_w[...] = jnp.zeros((64, 128), f32)
    hsf[...] = jnp.zeros((bands, 64, 128), f32)

    pl.semaphore_wait(barrier, strips - 1)

    def bit_copy(k):
        return pltpu.make_async_remote_copy(
            src_ref=words, dst_ref=bits.at[me], send_sem=bit_send.at[at(k)], recv_sem=bit_recv.at[me],
            device_id={"band": at(k)}, device_id_type=pl.DeviceIdType.MESH)

    def send_bits(k, c):
        bit_copy(k).start()
        return c

    lax.fori_loop(1, strips, send_bits, 0)
    own_bits = pltpu.make_async_copy(words, bits.at[me], own_sem.at[0])
    own_bits.start()

    load.wait()

    def first_rows(t, c):
        for s in range(bands):
            hsf[s, pl.ds(t, 1), :] = scn[t, s, 0:1, :].astype(f32)
        return c

    lax.fori_loop(0, dates, first_rows, 0, unroll=2)
    hs[...] = hsf[...].astype(bf16)
    halo = pltpu.make_async_remote_copy(
        src_ref=hs, dst_ref=hr, send_sem=halo_sem.at[0], recv_sem=halo_sem.at[1],
        device_id={"band": lax.rem(me + strips - 1, strips)}, device_id_type=pl.DeviceIdType.MESH)
    halo.start()

    def take_bits(k, c):
        pltpu.make_async_remote_copy(
            src_ref=words, dst_ref=bits.at[at(k)], send_sem=bit_send.at[at(k)], recv_sem=bit_recv.at[at(k)],
            device_id={"band": at(k)}, device_id_type=pl.DeviceIdType.MESH).wait()
        return c

    lax.fori_loop(1, strips, take_bits, 0)
    own_bits.wait()

    repeat = (lax.broadcasted_iota(i32, (128, strips), 0) // 4 == lax.broadcasted_iota(i32, (128, strips), 1)).astype(f32)
    cells = []
    for w in range(words.shape[0]):
        mine = pltpu.roll(bits[:, w, 0, :], lax.rem(8 * (strips - me), 8 * strips), 1)[:, :128]
        parts = []
        for piece in (mine & 32767, mine >> 15):
            spreadc = jnp.dot(repeat, piece.astype(f32), precision=lax.Precision.HIGHEST, preferred_element_type=f32)
            parts.append(spreadc.T[0:8].astype(i32))
        cells.append(parts[0] + parts[1] * 32768)

    def spread(cell, rb):
        return jnp.where(upper, cell[2 * rb : 2 * rb + 1, :], cell[2 * rb + 1 : 2 * rb + 2, :])

    for w in range(words.shape[0]):

        def date(j, c):
            t = 30 * w + j
            seen = (lane8 >= 4 * foot[0, t]) & (lane8 < 4 * foot[1, t] + 4)
            wt = jnp.where(seen, (cells[w] >> j) & 1, 0).astype(f32)
            fy = off[0, t].astype(f32) * 0.0625
            fx = off[1, t].astype(f32) * 0.0625
            edge_x[pl.ds(t, 1), :] = jnp.full((1, 128), fx)
            edge_w[pl.ds(t, 1), :] = wt[7:8, :] * fy
            for rb in range(4):
                wide[t, pl.ds(8 * rb, 8), :] = spread(wt, rb)
            cover[pl.ds(pl.multiple_of(8 * t, 8), 8), :] = wt
            return c

        lax.fori_loop(0, min(30, dates - 30 * w), date, 0, unroll=2)
    sums = jnp.dot(mix_gram[...], cover[...].astype(bf16), preferred_element_type=f32)
    acc = [sums[8 * n : 8 * n + 8] + sums[320 + 8 * n : 328 + 8 * n] for n in range(36)]
    acc += [sums[640 + 8 * m : 648 + 8 * m] for m in range(12)]
    gram = {}
    for i in range(8):
        for j in range(i + 1):
            gram[i, j] = acc[i * (i + 1) // 2 + j]
    low, inv = {}, {}
    for j in range(8):
        pivot = gram[j, j] + RIDGE
        for k in range(j):
            pivot = pivot - low[j, k] * low[j, k]
        inv[j] = 1.0 / jnp.sqrt(pivot)
        for i in range(j + 1, 8):
            run = gram[i, j]
            for k in range(j):
                run = run - low[i, k] * low[j, k]
            low[i, j] = run * inv[j]
    items = [inv[i] for i in range(8)]
    items += [low[i, j] for i in range(8) for j in range(i)]
    items += [1.0 / jnp.maximum(acc[36 + m], 1.0) for m in range(12)]
    total = acc[36]
    for m in range(1, 12):
        total = total + acc[36 + m]
    items.append(1.0 / jnp.maximum(total, 1.0))
    for n, item in enumerate(items):
        for rb in range(4):
            fac[n, pl.ds(8 * rb, 8), :] = spread(item, rb)

    halo.wait()

    @pl.when(me == strips - 1)
    def _():
        hr[...] = jnp.zeros((bands, 64, 128), bf16)

    lane = lax.broadcasted_iota(i32, (32, 128), 1)
    row = lax.broadcasted_iota(i32, (32, 128), 0)
    lane64 = lax.broadcasted_iota(i32, (64, 128), 1)
    ends = jnp.where(lane8 > 0, 0.25, 0.0), jnp.where(lane8 < 127, 0.25, 0.0)
    first = lax.broadcasted_iota(i32, (16, 8, 128), 1) < 4
    groups = send.shape[2] // 16

    def smooth(x):
        return 0.5 * x + ends[0] * pltpu.roll(x, 1, 1) + ends[1] * pltpu.roll(x, 127, 1)

    def band(s, carry):
        def pair(p, c):
            u = []
            for t2 in range(2):
                t = 2 * p + t2
                fy = off[0, t].astype(f32) * 0.0625
                fx = off[1, t].astype(f32) * 0.0625
                x = scn[t, s].astype(f32)
                xb = (1.0 - fx) * x + jnp.where(lane < 127, fx, 0.0) * pltpu.roll(x, 127, 1)
                v = (1.0 - fy) * xb + jnp.where(row < 31, fy, 0.0) * pltpu.roll(xb, 31, 0)
                u.append(v * wide[t])
            for rb in range(4):
                both = jnp.concatenate([u[0][8 * rb : 8 * rb + 8], u[1][8 * rb : 8 * rb + 8]], axis=0)
                stack[rb // 2, pl.ds(pl.multiple_of(16 * p, 16), 16), pl.ds(128 * (rb % 2), 128)] = both.astype(bf16)
            return c

        lax.fori_loop(0, dates // 2, pair, 0, unroll=2)
        e = hr[s].astype(f32)
        fx = edge_x[...]
        hu = ((1.0 - fx) * e + jnp.where(lane64 < 127, fx, 0.0) * pltpu.roll(e, 127, 1)) * edge_w[...]
        sums = [jnp.dot(mix[...], stack[h], preferred_element_type=f32) for h in range(2)]
        extra = jnp.dot(mix_last[...], hu.astype(bf16), preferred_element_type=f32)
        for rb in range(4):
            rows = pl.ds(8 * rb, 8)

            def term(n):
                part = sums[rb // 2][8 * n : 8 * n + 8, 128 * (rb % 2) : 128 * (rb % 2) + 128]
                return part + extra[8 * n : 8 * n + 8] if rb == 3 else part

            def fl(i, j):
                return fac[8 + i * (i - 1) // 2 + j, rows, :]

            def put(n, value):
                start = pl.multiple_of((s * 21 + n) * 32 + 8 * rb, 8)
                planes[pl.ds(start, 8), :] = value

            fwd = []
            for i in range(8):
                run = term(i) + term(8 + i)
                for k in range(i):
                    run = run - fl(i, k) * fwd[k]
                fwd.append(run * fac[i, rows, :])
            back = [None] * 8
            for i in reversed(range(8)):
                run = fwd[i]
                for k in range(i + 1, 8):
                    run = run - fl(k, i) * back[k]
                back[i] = run * fac[i, rows, :]
                put(i, back[i])
            whole = None
            for m in range(12):
                month = term(16 + m)
                whole = month if whole is None else whole + month
                put(8 + m, smooth(month * fac[36 + m, rows, :]))
            put(20, smooth(whole * fac[48, rows, :]))

        def group(gg, c):
            at16 = pl.ds(pl.multiple_of(16 * gg, 16), 16)
            halves = []
            for h in range(2):
                a, b = [
                    planes[pl.ds(pl.multiple_of((4 * gg + 2 * h + k) * 128, 128), 128), :].T.reshape(16, 8, 128)
                    for k in range(2)
                ]
                halves.append((jnp.where(first, a, pltpu.roll(b, 4, 1)), jnp.where(first, pltpu.roll(a, 4, 1), b)))
            for which in range(2):
                send[:, which, at16, :] = jnp.concatenate([halves[0][which], halves[1][which]], axis=1).astype(bf16)

            def push(k, c2):
                d = peer(k)
                pltpu.make_async_remote_copy(
                    src_ref=send.at[d // 2, d % 2, at16, :], dst_ref=out.at[me, at16, :],
                    send_sem=blk_send.at[d], recv_sem=blk_recv.at[me],
                    device_id={"band": d}, device_id_type=pl.DeviceIdType.MESH).start()
                return c2

            lax.fori_loop(0, half, push, 0)
            lax.fori_loop(half + 1, strips, push, 0)
            return c

        done = jnp.where(s == bands - 1, groups, (21 * (s + 1)) // 16)
        lax.fori_loop((21 * s) // 16, done, group, 0)
        return carry

    lax.fori_loop(0, bands, band, 0)
    own = pltpu.make_async_copy(send.at[me // 2, me % 2], out.at[me], own_sem.at[1])
    own.start()

    def finish(k, c):
        d = at(k)
        pltpu.make_async_remote_copy(
            src_ref=send.at[d // 2, d % 2], dst_ref=out.at[d], send_sem=blk_send.at[d], recv_sem=blk_recv.at[d],
            device_id={"band": d}, device_id_type=pl.DeviceIdType.MESH).wait()
        return c

    lax.fori_loop(1, strips, finish, 0)
    own.wait()


def lay_kernel(bands, recv, coef, monthly, annual, flat, sems):
    f32 = jnp.float32
    strips = recv.shape[0]
    quads = strips // 4
    width = strips * 32
    lane = lax.broadcasted_iota(jnp.int32, (8, 128), 1)
    even = (lane // 32) % 2 == 0
    front = lane < 64
    wide = lax.broadcasted_iota(jnp.int32, (8, width), 1)

    def swap(a, b, mask, shift):
        return jnp.where(mask, a, pltpu.roll(b, shift, 1)), jnp.where(mask, pltpu.roll(a, 128 - shift, 1), b)

    def rows8(gg, carry):
        rows = [[], [], [], []]
        for q in range(quads):
            v = [recv[4 * q + j, pl.ds(pl.multiple_of(8 * gg, 8), 8), :].astype(f32) for j in range(4)]
            a0, a1 = swap(v[0], v[1], even, 32)
            a2, a3 = swap(v[2], v[3], even, 32)
            o0, o2 = swap(a0, a2, front, 64)
            o1, o3 = swap(a1, a3, front, 64)
            for p, o in enumerate((o0, o1, o2, o3)):
                rows[p].append(o)
        for p in range(4):
            full = jnp.concatenate(rows[p], axis=1)
            before = jnp.where(wide > 0, pltpu.roll(full, 1, 1), 0.0)
            after = jnp.where(wide < width - 1, pltpu.roll(full, width - 1, 1), 0.0)
            soft = 0.25 * before + 0.5 * full + 0.25 * after
            for half in range(2):
                index = 8 * gg + 4 * half + p
                part = slice(4 * half, 4 * half + 4)
                flat[index] = jnp.where(index % 21 < 8, full[part], soft[part])

        def ship(n, c):
            index = 8 * gg + n
            s, j = index // 21, index % 21

            @pl.when((s < bands) & (j < 8))
            def _():
                pltpu.make_async_copy(flat.at[index], coef.at[j, s], sems.at[0]).start()

            @pl.when((s < bands) & (j >= 8) & (j < 20))
            def _():
                pltpu.make_async_copy(flat.at[index], monthly.at[j - 8, s], sems.at[1]).start()

            @pl.when((s < bands) & (j == 20))
            def _():
                pltpu.make_async_copy(flat.at[index], annual.at[s], sems.at[2]).start()

            return c

        lax.fori_loop(0, 8, ship, 0)
        return carry

    lax.fori_loop(0, recv.shape[1] // 8, rows8, 0)
    pltpu.make_async_copy(coef, coef, sems.at[0]).wait()
    pltpu.make_async_copy(monthly, monthly, sems.at[1]).wait()
    pltpu.make_async_copy(annual, annual, sems.at[2]).wait()


def fast(scenes, clear_bits, footprint, offsets, acq_day):
    f32, bf16 = jnp.float32, jnp.bfloat16
    dates, bands, rows, cols = scenes.shape
    strips = lax.axis_size("band")
    strip_width = cols // strips
    slots = -(-bands * 21 // 16) * 16
    smem = pl.BlockSpec(memory_space=pltpu.SMEM)
    vmem = pl.BlockSpec(memory_space=pltpu.VMEM)
    hbm = pl.BlockSpec(memory_space=pl.ANY)
    dma = pltpu.SemaphoreType.DMA
    recv = pl.pallas_call(
        functools.partial(fit_kernel, dates, bands, strips),
        out_shape=jax.ShapeDtypeStruct((strips, slots, cols), bf16),
        in_specs=[smem, smem, smem, vmem, hbm],
        out_specs=hbm,
        scratch_shapes=[
            pltpu.VMEM((dates, bands, rows, cols), bf16),
            pltpu.VMEM((bands, 64, cols), f32),
            pltpu.VMEM((bands, 64, cols), bf16),
            pltpu.VMEM((bands, 64, cols), bf16),
            pltpu.VMEM((strips,) + clear_bits.shape, jnp.int32),
            pltpu.VMEM((224, dates * 8), bf16),
            pltpu.VMEM((224, 64), bf16),
            pltpu.VMEM((dates, rows, cols), f32),
            pltpu.VMEM((768, dates * 8), bf16),
            pltpu.VMEM((dates * 8, cols), f32),
            pltpu.VMEM((64, cols), f32),
            pltpu.VMEM((64, cols), f32),
            pltpu.VMEM((49, rows, cols), f32),
            pltpu.VMEM((2, dates * 8, 2 * cols), bf16),
            pltpu.VMEM((slots * rows, cols), f32),
            pltpu.VMEM((strips // 2, 2, slots, cols), bf16),
            dma, dma((strips,)), dma((strips,)), dma((2,)), dma((strips,)), dma((strips,)), dma((2,)),
        ],
        compiler_params=pltpu.CompilerParams(collective_id=0, has_side_effects=True, vmem_limit_bytes=58 * 1024 * 1024),
    )(offsets.T, footprint.T, acq_day, clear_bits, scenes)
    return pl.pallas_call(
        functools.partial(lay_kernel, bands),
        out_shape=(
            jax.ShapeDtypeStruct((8, bands, strip_width, rows * strips), f32),
            jax.ShapeDtypeStruct((12, bands, strip_width, rows * strips), f32),
            jax.ShapeDtypeStruct((bands, strip_width, rows * strips), f32),
        ),
        in_specs=[vmem],
        out_specs=(hbm, hbm, hbm),
        scratch_shapes=[
            pltpu.VMEM((slots, strip_width, rows * strips), f32),
            dma((3,)),
        ],
        compiler_params=pltpu.CompilerParams(vmem_limit_bytes=56 * 1024 * 1024),
    )(recv)


def pick(scenes, clear_bits, footprint, offsets, acq_day):
    dates, bands, rows, cols = scenes.shape
    strips = lax.axis_size("band")
    fits = lax.axis_size("tile") == 1 and lax.axis_size("sub") == 1 and strips % 4 == 0
    fits = fits and cols == 128 and rows == 32 and cols == 4 * strips and dates % 2 == 0 and dates <= 60
    return (fast if fits else shards)(scenes, clear_bits, footprint, offsets, acq_day)


def solution(mesh):
    placed = (
        P(("region", "tile"), "sub", "band", None),
        P(("region", "tile"), "band", None),
        P(("region", "tile"), None),
        P(("region", "tile"), None),
        P(("region", "tile")),
    )
    return jax.shard_map(
        pick,
        mesh=mesh,
        in_specs=placed,
        out_specs=(
            P("region", "sub", "band", "tile"),
            P(("region", "tile"), "sub", "band", None),
            P(("region", "sub"), "band", "tile"),
        ),
        check_vma=False,
    )
```

```python
import functools
import math

import jax
import jax.numpy as jnp
from jax import lax
from jax.experimental import pallas as pl
from jax.experimental.pallas import tpu as pltpu
from jax.sharding import PartitionSpec as P

RIDGE = 1.0


def shifted(value, axis, steps):
    count = lax.axis_size(axis)
    first, last = (max(0, -steps), min(count, count - steps))
    return lax.ppermute(value, axis, [(source, source + steps) for source in range(first, last)])


def extended(x, sides, width):
    for axis, dim in sides:
        devices, length = (lax.axis_size(axis), x.shape[dim])
        up = [(i, (i + 1) % devices) for i in range(devices - 1)]
        down = [(j, i) for i, j in up]
        last = lax.slice_in_dim(x, length - width, length, axis=dim)
        first = lax.slice_in_dim(x, 0, width, axis=dim)
        before = lax.ppermute(last, axis, up)
        after = lax.ppermute(first, axis, down)
        x = jnp.concatenate([before, x, after], axis=dim)
    return x


def design_tables(acq_day):
    day_phase = acq_day.astype(jnp.float32) / 365.0
    columns = [jnp.ones_like(day_phase), 2.0 * day_phase - 1.0]
    for harmonic in (1, 2, 3):
        turn_angle = 2.0 * jnp.pi * harmonic * day_phase
        columns = columns + [jnp.cos(turn_angle), jnp.sin(turn_angle)]
    harmonic_basis = jnp.stack(columns, axis=1)
    month_index = acq_day * 12 // 365
    onehot = (month_index[:, None] == jnp.arange(12, dtype=jnp.int32)[None, :]).astype(jnp.float32)
    products = jnp.stack(
        [
            harmonic_basis[:, row_term] * harmonic_basis[:, col_term]
            for row_term in range(8)
            for col_term in range(row_term + 1)
        ],
        axis=1,
    )
    return (
        jnp.concatenate([products, onehot], axis=1),
        jnp.concatenate([harmonic_basis, onehot], axis=1),
    )


def bilinear(padded, offsets):
    shift_row = (offsets[:, 0].astype(jnp.float32) / 16.0)[:, None, None, None]
    shift_col = (offsets[:, 1].astype(jnp.float32) / 16.0)[:, None, None, None]
    upper_rows = padded[:, :, :-1].astype(jnp.float32)
    lower_rows = padded[:, :, 1:].astype(jnp.float32)

    def across(source):
        right_cell = jnp.concatenate([source[..., 1:], jnp.zeros_like(source[..., :1])], axis=-1)
        return (1.0 - shift_col) * source + shift_col * right_cell

    return ((1.0 - shift_row) * across(upper_rows) + shift_row * across(lower_rows)).astype(
        jnp.bfloat16
    )


def clear_weight(cell_words, footprint, strip_width):
    date_count = footprint.shape[0]
    per_date = jnp.repeat(cell_words, 30, axis=0)
    bit_place = (jnp.arange(date_count, dtype=jnp.int32) % 30)[:, None, None]
    clear_flag = jnp.right_shift(per_date, bit_place) & 1
    pixel_flag = jnp.repeat(jnp.repeat(clear_flag, 4, axis=1), 4, axis=2)
    strip_index = jnp.arange(pixel_flag.shape[1], dtype=jnp.int32) // strip_width
    covered = (strip_index[None, :] >= footprint[:, 0:1]) & (
        strip_index[None, :] <= footprint[:, 1:2]
    )
    return pixel_flag.astype(jnp.float32) * covered[:, :, None].astype(jnp.float32)


def partial_sums(weight, values, common_table, banded_table):
    common = jnp.einsum("dxy,dk->kxy", weight, common_table, precision=lax.Precision.HIGHEST)
    weighted = values.astype(jnp.float32) * weight[:, None]
    banded = jnp.einsum("dsxy,dk->ksxy", weighted, banded_table, precision=lax.Precision.HIGHEST)
    return (common, banded)


def solve_normal(gram, rhs):
    pair_list = [(row_term, col_term) for row_term in range(8) for col_term in range(row_term + 1)]
    gram_entry = {}
    for position, term_pair in enumerate(pair_list):
        gram_entry[term_pair] = gram[position]
    factor = {}
    for col_term in range(8):
        pivot_value = gram_entry[col_term, col_term] + RIDGE
        for inner_term in range(col_term):
            pivot_value = pivot_value - factor[col_term, inner_term] * factor[col_term, inner_term]
        diag_root = jnp.sqrt(pivot_value)
        factor[col_term, col_term] = diag_root
        for row_term in range(col_term + 1, 8):
            running = gram_entry[row_term, col_term]
            for inner_term in range(col_term):
                running = running - factor[row_term, inner_term] * factor[col_term, inner_term]
            factor[row_term, col_term] = running / diag_root
    forward = []
    for row_term in range(8):
        running = rhs[row_term]
        for inner_term in range(row_term):
            running = running - factor[row_term, inner_term] * forward[inner_term]
        forward.append(running / factor[row_term, row_term])
    backward = [forward[0]] * 8
    for row_term in reversed(range(8)):
        running = forward[row_term]
        for inner_term in range(row_term + 1, 8):
            running = running - factor[inner_term, row_term] * backward[inner_term]
        backward[row_term] = running / factor[row_term, row_term]
    return jnp.stack(backward, axis=0)


def smooth_axis(padded_field, along):
    inner_size = padded_field.shape[along] - 2
    left_part = lax.slice_in_dim(padded_field, 0, inner_size, axis=along)
    centre_part = lax.slice_in_dim(padded_field, 1, inner_size + 1, axis=along)
    right_part = lax.slice_in_dim(padded_field, 2, inner_size + 2, axis=along)
    return 0.25 * left_part + 0.5 * centre_part + 0.25 * right_part


def shards(scenes, clear_bits, footprint, offsets, acq_day):
    date_count, band_count, row_local, col_count = scenes.shape
    strip_count = lax.axis_size("band")
    tile_count = lax.axis_size("tile")
    strip_width = col_count // strip_count
    row_count = row_local * strip_count
    common_table, banded_table = design_tables(acq_day)
    below = shifted(scenes[:, :, 0:1, :], "band", -1)
    resampled = bilinear(jnp.concatenate([scenes, below], axis=2), offsets)
    flipped = jnp.swapaxes(resampled, 2, 3)
    cell_words = lax.all_to_all(clear_bits, "band", split_axis=2, concat_axis=1, tiled=True)
    weight = clear_weight(cell_words, footprint, strip_width)
    common, banded = partial_sums(weight, flipped, common_table, banded_table)
    common, banded = (
        lax.all_to_all(common, "band", split_axis=1, concat_axis=2, tiled=True),
        lax.all_to_all(
            banded.reshape(-1, col_count, row_local),
            "band",
            split_axis=1,
            concat_axis=2,
            tiled=True,
        ),
    )
    banded = banded.reshape(20, band_count, strip_width, row_count)
    gram = common[:36]
    month_count = common[36:]
    rhs = banded[:8]
    month_sum = banded[8:]
    annual_sum = jnp.sum(month_sum, axis=0)
    annual_count = jnp.sum(month_count, axis=0)
    month_sum, month_count = (
        lax.psum_scatter(month_sum, "tile", scatter_dimension=0, tiled=True),
        lax.psum_scatter(month_count, "tile", scatter_dimension=0, tiled=True),
    )
    composite = month_sum / jnp.maximum(month_count, 1.0)[:, None]
    month_edged = extended(composite, (("band", 2),), 1)
    month_edged = jnp.pad(month_edged, ((0, 0), (0, 0), (0, 0), (1, 1)))
    monthly = smooth_axis(smooth_axis(month_edged, 3), 2)
    share = row_count // tile_count
    gram, rhs, annual_sum, annual_count = lax.psum((gram, rhs, annual_sum, annual_count), "tile")
    start = lax.axis_index("tile") * share
    gram = lax.dynamic_slice_in_dim(gram, start, share, 2)
    rhs = lax.dynamic_slice_in_dim(rhs, start, share, 3)
    annual_sum = lax.dynamic_slice_in_dim(annual_sum, start, share, 2)
    annual_count = lax.dynamic_slice_in_dim(annual_count, start, share, 1)
    coefficients = solve_normal(gram, rhs)
    yearly = annual_sum / jnp.maximum(annual_count, 1.0)
    year_edged = extended(yearly, (("band", 1), ("tile", 2)), 1)
    annual = smooth_axis(smooth_axis(year_edged, 2), 1)
    return (coefficients, monthly, annual)


def fit_kernel(dates, bands, strips, off, foot, day_s, words, scenes, out,
               scn, hsf, hs, hr, bits, mix, mix_last, wide, mix_gram, cover, edge_x, edge_w, fac, stack, planes, send,
               scene_sem, bit_send, bit_recv, halo_sem, blk_send, blk_recv, own_sem):
    f32, bf16, i32 = jnp.float32, jnp.bfloat16, jnp.int32
    me = lax.axis_index("band")
    sub8 = lax.broadcasted_iota(i32, (8, 128), 0)
    lane8 = lax.broadcasted_iota(i32, (8, 128), 1)
    upper = sub8 < 4
    depth = dates * 8
    load = pltpu.make_async_copy(scenes, scn, scene_sem)
    load.start()

    def at(k):
        return lax.rem(me + k, strips)

    half = strips // 2

    def peer(k):
        cross = (me // half + 1 + k // half) % 2
        return cross * half + (me + k) % half

    barrier = pltpu.get_barrier_semaphore()

    def greet(k, c):
        pl.semaphore_signal(barrier, inc=1, device_id={"band": at(k)}, device_id_type=pl.DeviceIdType.MESH)
        return c

    lax.fori_loop(1, strips, greet, 0)

    def basis(day, which):
        u = day.astype(f32) / 365.0
        turn = (which // 2).astype(f32) * u - jnp.where(which % 2 == 1, 0.25, 0.0)
        turn = turn - jnp.floor(turn + 0.5)
        square = (turn * turn) * (4.0 * math.pi * math.pi)
        wave = jnp.full_like(square, 1.0 / math.factorial(20))
        for k in range(9, -1, -1):
            wave = (-1.0) ** k / math.factorial(2 * k) + wave * square
        return jnp.where(which == 0, 1.0, jnp.where(which == 1, 2.0 * u - 1.0, wave))

    lane64i = lax.broadcasted_iota(i32, (16, 64), 1)

    def days(t, acc):
        return jnp.where(lane64i == t, day_s[t], acc)

    day64 = lax.fori_loop(0, dates, days, jnp.zeros((16, 64), i32), unroll=10)
    d8 = day64[0:8]
    which8 = lax.broadcasted_iota(i32, (8, 64), 0)
    real = lax.broadcasted_iota(i32, (8, 64), 1) < dates
    b8 = jnp.where(real, basis(d8, which8), 0.0)
    high = b8.astype(bf16).astype(f32)
    d16 = day64 * 12
    m16 = lax.broadcasted_iota(i32, (16, 64), 0)
    ok16 = (lax.broadcasted_iota(i32, (16, 64), 1) < dates) & (m16 < 12)
    hot = jnp.where(ok16 & (d16 >= 365 * m16) & (d16 < 365 * m16 + 365), 1.0, 0.0)
    tab_in = jnp.concatenate([high, b8 - high, hot], axis=0).astype(bf16)
    choose = (lax.broadcasted_iota(i32, (224, 32), 0) // 8 == lax.broadcasted_iota(i32, (224, 32), 1)).astype(f32).astype(bf16)
    tab = jnp.dot(choose, tab_in, preferred_element_type=f32)
    last = lax.broadcasted_iota(i32, (224, 64), 0) % 8 == 7
    mix_last[...] = jnp.where(last, tab, 0.0).astype(bf16)
    place = (lax.broadcasted_iota(i32, (64, depth), 1) // 8 == lax.broadcasted_iota(i32, (64, depth), 0)).astype(f32).astype(bf16)
    full = jnp.dot(tab.astype(bf16), place, preferred_element_type=f32)
    same = lax.broadcasted_iota(i32, (224, depth), 0) % 8 == lax.broadcasted_iota(i32, (224, depth), 1) % 8
    mix[...] = jnp.where(same, full, 0.0).astype(bf16)
    pairs = jnp.concatenate([b8[i : i + 1] * b8[: i + 1] for i in range(8)] + [jnp.zeros((4, 64), f32)], axis=0)
    high_pairs = pairs.astype(bf16).astype(f32)
    tab_pairs = jnp.concatenate([high_pairs, pairs - high_pairs, hot], axis=0).astype(bf16)
    choose = (lax.broadcasted_iota(i32, (768, 96), 0) // 8 == lax.broadcasted_iota(i32, (768, 96), 1)).astype(f32).astype(bf16)
    tab = jnp.dot(choose, tab_pairs, preferred_element_type=f32)
    full = jnp.dot(tab.astype(bf16), place, preferred_element_type=f32)
    same = lax.broadcasted_iota(i32, (768, depth), 0) % 8 == lax.broadcasted_iota(i32, (768, depth), 1) % 8
    mix_gram[...] = jnp.where(same, full, 0.0).astype(bf16)
    planes[pl.ds(bands * 21 * 32, 64), :] = jnp.zeros((64, 128), f32)
    edge_x[...] = jnp.zeros((64, 128), f32)
    edge_w[...] = jnp.zeros((64, 128), f32)
    hsf[...] = jnp.zeros((bands, 64, 128), f32)

    pl.semaphore_wait(barrier, strips - 1)

    def bit_copy(k):
        return pltpu.make_async_remote_copy(
            src_ref=words, dst_ref=bits.at[me], send_sem=bit_send.at[at(k)], recv_sem=bit_recv.at[me],
            device_id={"band": at(k)}, device_id_type=pl.DeviceIdType.MESH)

    def send_bits(k, c):
        bit_copy(k).start()
        return c

    lax.fori_loop(1, strips, send_bits, 0)
    own_bits = pltpu.make_async_copy(words, bits.at[me], own_sem.at[0])
    own_bits.start()

    load.wait()

    def first_rows(t, c):
        for s in range(bands):
            hsf[s, pl.ds(t, 1), :] = scn[t, s, 0:1, :].astype(f32)
        return c

    lax.fori_loop(0, dates, first_rows, 0, unroll=2)
    hs[...] = hsf[...].astype(bf16)
    halo = pltpu.make_async_remote_copy(
        src_ref=hs, dst_ref=hr, send_sem=halo_sem.at[0], recv_sem=halo_sem.at[1],
        device_id={"band": lax.rem(me + strips - 1, strips)}, device_id_type=pl.DeviceIdType.MESH)
    halo.start()

    def take_bits(k, c):
        pltpu.make_async_remote_copy(
            src_ref=words, dst_ref=bits.at[at(k)], send_sem=bit_send.at[at(k)], recv_sem=bit_recv.at[at(k)],
            device_id={"band": at(k)}, device_id_type=pl.DeviceIdType.MESH).wait()
        return c

    lax.fori_loop(1, strips, take_bits, 0)
    own_bits.wait()

    repeat = (lax.broadcasted_iota(i32, (128, strips), 0) // 4 == lax.broadcasted_iota(i32, (128, strips), 1)).astype(f32)
    cells = []
    for w in range(words.shape[0]):
        mine = pltpu.roll(bits[:, w, 0, :], lax.rem(8 * (strips - me), 8 * strips), 1)[:, :128]
        parts = []
        for piece in (mine & 32767, mine >> 15):
            spreadc = jnp.dot(repeat, piece.astype(f32), precision=lax.Precision.HIGHEST, preferred_element_type=f32)
            parts.append(spreadc.T[0:8].astype(i32))
        cells.append(parts[0] + parts[1] * 32768)

    def spread(cell, rb):
        return jnp.where(upper, cell[2 * rb : 2 * rb + 1, :], cell[2 * rb + 1 : 2 * rb + 2, :])

    for w in range(words.shape[0]):

        def date(j, c):
            t = 30 * w + j
            seen = (lane8 >= 4 * foot[0, t]) & (lane8 < 4 * foot[1, t] + 4)
            wt = jnp.where(seen, (cells[w] >> j) & 1, 0).astype(f32)
            fy = off[0, t].astype(f32) * 0.0625
            fx = off[1, t].astype(f32) * 0.0625
            edge_x[pl.ds(t, 1), :] = jnp.full((1, 128), fx)
            edge_w[pl.ds(t, 1), :] = wt[7:8, :] * fy
            for rb in range(4):
                wide[t, pl.ds(8 * rb, 8), :] = spread(wt, rb)
            cover[pl.ds(pl.multiple_of(8 * t, 8), 8), :] = wt
            return c

        lax.fori_loop(0, min(30, dates - 30 * w), date, 0, unroll=2)
    sums = jnp.dot(mix_gram[...], cover[...].astype(bf16), preferred_element_type=f32)
    acc = [sums[8 * n : 8 * n + 8] + sums[320 + 8 * n : 328 + 8 * n] for n in range(36)]
    acc += [sums[640 + 8 * m : 648 + 8 * m] for m in range(12)]
    gram = {}
    for i in range(8):
        for j in range(i + 1):
            gram[i, j] = acc[i * (i + 1) // 2 + j]
    low, inv = {}, {}
    for j in range(8):
        pivot = gram[j, j] + RIDGE
        for k in range(j):
            pivot = pivot - low[j, k] * low[j, k]
        inv[j] = 1.0 / jnp.sqrt(pivot)
        for i in range(j + 1, 8):
            run = gram[i, j]
            for k in range(j):
                run = run - low[i, k] * low[j, k]
            low[i, j] = run * inv[j]
    items = [inv[i] for i in range(8)]
    items += [low[i, j] for i in range(8) for j in range(i)]
    items += [1.0 / jnp.maximum(acc[36 + m], 1.0) for m in range(12)]
    total = acc[36]
    for m in range(1, 12):
        total = total + acc[36 + m]
    items.append(1.0 / jnp.maximum(total, 1.0))
    for n, item in enumerate(items):
        for rb in range(4):
            fac[n, pl.ds(8 * rb, 8), :] = spread(item, rb)

    halo.wait()

    @pl.when(me == strips - 1)
    def _():
        hr[...] = jnp.zeros((bands, 64, 128), bf16)

    lane = lax.broadcasted_iota(i32, (32, 128), 1)
    row = lax.broadcasted_iota(i32, (32, 128), 0)
    lane64 = lax.broadcasted_iota(i32, (64, 128), 1)
    ends = jnp.where(lane8 > 0, 0.25, 0.0), jnp.where(lane8 < 127, 0.25, 0.0)
    first = lax.broadcasted_iota(i32, (16, 8, 128), 1) < 4
    groups = send.shape[2] // 16

    def smooth(x):
        return 0.5 * x + ends[0] * pltpu.roll(x, 1, 1) + ends[1] * pltpu.roll(x, 127, 1)

    def band(s, carry):
        def pair(p, c):
            u = []
            for t2 in range(2):
                t = 2 * p + t2
                fy = off[0, t].astype(f32) * 0.0625
                fx = off[1, t].astype(f32) * 0.0625
                x = scn[t, s].astype(f32)
                xb = (1.0 - fx) * x + jnp.where(lane < 127, fx, 0.0) * pltpu.roll(x, 127, 1)
                v = (1.0 - fy) * xb + jnp.where(row < 31, fy, 0.0) * pltpu.roll(xb, 31, 0)
                u.append(v * wide[t])
            for rb in range(4):
                both = jnp.concatenate([u[0][8 * rb : 8 * rb + 8], u[1][8 * rb : 8 * rb + 8]], axis=0)
                stack[rb // 2, pl.ds(pl.multiple_of(16 * p, 16), 16), pl.ds(128 * (rb % 2), 128)] = both.astype(bf16)
            return c

        lax.fori_loop(0, dates // 2, pair, 0, unroll=2)
        e = hr[s].astype(f32)
        fx = edge_x[...]
        hu = ((1.0 - fx) * e + jnp.where(lane64 < 127, fx, 0.0) * pltpu.roll(e, 127, 1)) * edge_w[...]
        sums = [jnp.dot(mix[...], stack[h], preferred_element_type=f32) for h in range(2)]
        extra = jnp.dot(mix_last[...], hu.astype(bf16), preferred_element_type=f32)
        for rb in range(4):
            rows = pl.ds(8 * rb, 8)

            def term(n):
                part = sums[rb // 2][8 * n : 8 * n + 8, 128 * (rb % 2) : 128 * (rb % 2) + 128]
                return part + extra[8 * n : 8 * n + 8] if rb == 3 else part

            def fl(i, j):
                return fac[8 + i * (i - 1) // 2 + j, rows, :]

            def put(n, value):
                start = pl.multiple_of((s * 21 + n) * 32 + 8 * rb, 8)
                planes[pl.ds(start, 8), :] = value

            fwd = []
            for i in range(8):
                run = term(i) + term(8 + i)
                for k in range(i):
                    run = run - fl(i, k) * fwd[k]
                fwd.append(run * fac[i, rows, :])
            back = [None] * 8
            for i in reversed(range(8)):
                run = fwd[i]
                for k in range(i + 1, 8):
                    run = run - fl(k, i) * back[k]
                back[i] = run * fac[i, rows, :]
                put(i, back[i])
            whole = None
            for m in range(12):
                month = term(16 + m)
                whole = month if whole is None else whole + month
                put(8 + m, smooth(month * fac[36 + m, rows, :]))
            put(20, smooth(whole * fac[48, rows, :]))

        def group(gg, c):
            at16 = pl.ds(pl.multiple_of(16 * gg, 16), 16)
            halves = []
            for h in range(2):
                a, b = [
                    planes[pl.ds(pl.multiple_of((4 * gg + 2 * h + k) * 128, 128), 128), :].T.reshape(16, 8, 128)
                    for k in range(2)
                ]
                halves.append((jnp.where(first, a, pltpu.roll(b, 4, 1)), jnp.where(first, pltpu.roll(a, 4, 1), b)))
            for which in range(2):
                send[:, which, at16, :] = jnp.concatenate([halves[0][which], halves[1][which]], axis=1).astype(bf16)

            def push(k, c2):
                d = peer(k)
                pltpu.make_async_remote_copy(
                    src_ref=send.at[d // 2, d % 2, at16, :], dst_ref=out.at[me, at16, :],
                    send_sem=blk_send.at[d], recv_sem=blk_recv.at[me],
                    device_id={"band": d}, device_id_type=pl.DeviceIdType.MESH).start()
                return c2

            lax.fori_loop(0, half, push, 0)
            return c

        done = jnp.where(s == bands - 1, groups, (21 * (s + 1)) // 16)
        lax.fori_loop((21 * s) // 16, done, group, 0)
        return carry

    lax.fori_loop(0, bands, band, 0)

    def push_near(k, c):
        d = peer(k)
        pltpu.make_async_remote_copy(
            src_ref=send.at[d // 2, d % 2], dst_ref=out.at[me], send_sem=blk_send.at[d], recv_sem=blk_recv.at[me],
            device_id={"band": d}, device_id_type=pl.DeviceIdType.MESH).start()
        return c

    lax.fori_loop(half + 1, strips, push_near, 0)
    own = pltpu.make_async_copy(send.at[me // 2, me % 2], out.at[me], own_sem.at[1])
    own.start()

    def finish(k, c):
        d = at(k)
        pltpu.make_async_remote_copy(
            src_ref=send.at[d // 2, d % 2], dst_ref=out.at[d], send_sem=blk_send.at[d], recv_sem=blk_recv.at[d],
            device_id={"band": d}, device_id_type=pl.DeviceIdType.MESH).wait()
        return c

    lax.fori_loop(1, strips, finish, 0)
    own.wait()


def lay_kernel(bands, recv, coef, monthly, annual, flat, sems):
    f32 = jnp.float32
    strips = recv.shape[0]
    quads = strips // 4
    width = strips * 32
    lane = lax.broadcasted_iota(jnp.int32, (8, 128), 1)
    even = (lane // 32) % 2 == 0
    front = lane < 64
    wide = lax.broadcasted_iota(jnp.int32, (8, width), 1)

    def swap(a, b, mask, shift):
        return jnp.where(mask, a, pltpu.roll(b, shift, 1)), jnp.where(mask, pltpu.roll(a, 128 - shift, 1), b)

    def rows8(gg, carry):
        rows = [[], [], [], []]
        for q in range(quads):
            v = [recv[4 * q + j, pl.ds(pl.multiple_of(8 * gg, 8), 8), :].astype(f32) for j in range(4)]
            a0, a1 = swap(v[0], v[1], even, 32)
            a2, a3 = swap(v[2], v[3], even, 32)
            o0, o2 = swap(a0, a2, front, 64)
            o1, o3 = swap(a1, a3, front, 64)
            for p, o in enumerate((o0, o1, o2, o3)):
                rows[p].append(o)
        for p in range(4):
            full = jnp.concatenate(rows[p], axis=1)
            before = jnp.where(wide > 0, pltpu.roll(full, 1, 1), 0.0)
            after = jnp.where(wide < width - 1, pltpu.roll(full, width - 1, 1), 0.0)
            soft = 0.25 * before + 0.5 * full + 0.25 * after
            for half in range(2):
                index = 8 * gg + 4 * half + p
                part = slice(4 * half, 4 * half + 4)
                flat[index] = jnp.where(index % 21 < 8, full[part], soft[part])

        def ship(n, c):
            index = 8 * gg + n
            s, j = index // 21, index % 21

            @pl.when((s < bands) & (j < 8))
            def _():
                pltpu.make_async_copy(flat.at[index], coef.at[j, s], sems.at[0]).start()

            @pl.when((s < bands) & (j >= 8) & (j < 20))
            def _():
                pltpu.make_async_copy(flat.at[index], monthly.at[j - 8, s], sems.at[1]).start()

            @pl.when((s < bands) & (j == 20))
            def _():
                pltpu.make_async_copy(flat.at[index], annual.at[s], sems.at[2]).start()

            return c

        lax.fori_loop(0, 8, ship, 0)
        return carry

    lax.fori_loop(0, recv.shape[1] // 8, rows8, 0)
    pltpu.make_async_copy(coef, coef, sems.at[0]).wait()
    pltpu.make_async_copy(monthly, monthly, sems.at[1]).wait()
    pltpu.make_async_copy(annual, annual, sems.at[2]).wait()


def fast(scenes, clear_bits, footprint, offsets, acq_day):
    f32, bf16 = jnp.float32, jnp.bfloat16
    dates, bands, rows, cols = scenes.shape
    strips = lax.axis_size("band")
    strip_width = cols // strips
    slots = -(-bands * 21 // 16) * 16
    smem = pl.BlockSpec(memory_space=pltpu.SMEM)
    vmem = pl.BlockSpec(memory_space=pltpu.VMEM)
    hbm = pl.BlockSpec(memory_space=pl.ANY)
    dma = pltpu.SemaphoreType.DMA
    recv = pl.pallas_call(
        functools.partial(fit_kernel, dates, bands, strips),
        out_shape=jax.ShapeDtypeStruct((strips, slots, cols), bf16),
        in_specs=[smem, smem, smem, vmem, hbm],
        out_specs=hbm,
        scratch_shapes=[
            pltpu.VMEM((dates, bands, rows, cols), bf16),
            pltpu.VMEM((bands, 64, cols), f32),
            pltpu.VMEM((bands, 64, cols), bf16),
            pltpu.VMEM((bands, 64, cols), bf16),
            pltpu.VMEM((strips,) + clear_bits.shape, jnp.int32),
            pltpu.VMEM((224, dates * 8), bf16),
            pltpu.VMEM((224, 64), bf16),
            pltpu.VMEM((dates, rows, cols), f32),
            pltpu.VMEM((768, dates * 8), bf16),
            pltpu.VMEM((dates * 8, cols), f32),
            pltpu.VMEM((64, cols), f32),
            pltpu.VMEM((64, cols), f32),
            pltpu.VMEM((49, rows, cols), f32),
            pltpu.VMEM((2, dates * 8, 2 * cols), bf16),
            pltpu.VMEM((slots * rows, cols), f32),
            pltpu.VMEM((strips // 2, 2, slots, cols), bf16),
            dma, dma((strips,)), dma((strips,)), dma((2,)), dma((strips,)), dma((strips,)), dma((2,)),
        ],
        compiler_params=pltpu.CompilerParams(collective_id=0, has_side_effects=True, vmem_limit_bytes=58 * 1024 * 1024),
    )(offsets.T, footprint.T, acq_day, clear_bits, scenes)
    return pl.pallas_call(
        functools.partial(lay_kernel, bands),
        out_shape=(
            jax.ShapeDtypeStruct((8, bands, strip_width, rows * strips), f32),
            jax.ShapeDtypeStruct((12, bands, strip_width, rows * strips), f32),
            jax.ShapeDtypeStruct((bands, strip_width, rows * strips), f32),
        ),
        in_specs=[vmem],
        out_specs=(hbm, hbm, hbm),
        scratch_shapes=[
            pltpu.VMEM((slots, strip_width, rows * strips), f32),
            dma((3,)),
        ],
        compiler_params=pltpu.CompilerParams(vmem_limit_bytes=56 * 1024 * 1024),
    )(recv)


def pick(scenes, clear_bits, footprint, offsets, acq_day):
    dates, bands, rows, cols = scenes.shape
    strips = lax.axis_size("band")
    fits = lax.axis_size("tile") == 1 and lax.axis_size("sub") == 1 and strips % 4 == 0
    fits = fits and cols == 128 and rows == 32 and cols == 4 * strips and dates % 2 == 0 and dates <= 60
    return (fast if fits else shards)(scenes, clear_bits, footprint, offsets, acq_day)


def solution(mesh):
    placed = (
        P(("region", "tile"), "sub", "band", None),
        P(("region", "tile"), "band", None),
        P(("region", "tile"), None),
        P(("region", "tile"), None),
        P(("region", "tile")),
    )
    return jax.shard_map(
        pick,
        mesh=mesh,
        in_specs=placed,
        out_specs=(
            P("region", "sub", "band", "tile"),
            P(("region", "tile"), "sub", "band", None),
            P(("region", "sub"), "band", "tile"),
        ),
        check_vma=False,
    )
```
